32 devices in a mesh: macro: 16 (over z, x, core), vox: 2 (over y).
Axes of the slice: x: 2, y: 2, z: 4, core: 2. Of those that a mesh axis runs over, the one named last changes fastest.
Arguments:
- displacement: float32 [3, 1024], P(None, 'macro'), may hold values from -1.2 to 1.2
- load: float32 [3, 1024], P(None, 'macro'), may hold values from -6 to 6
- conn: int32 [8, 1024], P(None, 'macro'), may hold values from 0 to 79
- halo_list: int32 [256], P('macro'), may hold values from 0 to 63
- grad_ops: float32 [3, 8, 1024], P(None, None, 'macro'), may hold values from -3 to 3
- volume: float32 [1024], P('macro'), may hold values from 0.5 to 2
- elastic_moduli: float32 [2, 1024], P(None, 'macro'), may hold values from 1 to 4
- plastic_mask: int32 [1024], P('macro'), may hold values from 0 to 1, as said below
- new_owner: int32 [1024], P('macro'), may hold values from -1 to 15, as said below
- state: float32 [7, 1024, 16, 256], P(None, 'macro', 'vox'), may hold values from -0.6 to 1, as said below
- micro_moduli: float32 [4, 16, 256], P(None, 'vox'), may hold values from 0.5 to 6
Outputs:
- residual: float32 [3, 1024], P(None, 'macro')
- moved_state: float32 [7, 384, 16, 256], P(None, 'macro', 'vox')
The draws below stay inside these ranges and needn't reach their ends.
Inputs may be any that keep to these rules, and one draw needn't show every extreme that they name: `plastic_mask`: each group's 64 points hold at most 48 plastic ones, 384 in all. `new_owner`: -1 exactly at elastic points; every group becomes the owner of exactly 24 plastic points, at most 3 of them from any one group. `state`: component 6 is nonnegative.
All inputs are finite; a program needn't handle non-finite values.
Results may differ from the reference program's by a relative error of at most 0.0001.
Values sent between devices are 32-bit elements; how exact they have to be, the bound alone decides.
A program may use at most 64 MiB of HBM per device.

```python
import math
import jax
import jax.numpy as jnp
from jax import lax

GROUPS = 16
ELEM_DEV = 64
NODE_DEV = 64
HALO_NODES = 16
RECV_AGG = 24
VOX_SIDE = 16
VOX_PLANE = 256
SWEEPS = 4


def owner_plan(key):
    folded = jax.random.fold_in(key, 7)
    key_count, key_pick, key_dest = jax.random.split(folded, 3)
    middle = GROUPS // 2
    levels = jnp.arange(middle, dtype=jnp.int32)
    spread = RECV_AGG * levels // (middle - 1)
    counts = jnp.concatenate([RECV_AGG + spread, RECV_AGG - spread])
    counts = counts[jax.random.permutation(key_count, GROUPS)]
    orders = jax.vmap(lambda k: jax.random.permutation(k, ELEM_DEV))(jax.random.split(key_pick, GROUPS))
    ranking = jnp.argsort(orders, axis=1)
    plastic = (ranking < counts[:, None]).reshape(-1)
    running = jnp.cumsum(plastic.astype(jnp.int32)) - 1
    targets = jax.random.permutation(key_dest, GROUPS).astype(jnp.int32)
    owners = targets[running % GROUPS]
    return (plastic.astype(jnp.int32), jnp.where(plastic, owners, -1).astype(jnp.int32))


def draw_plastic_mask(key, part):
    return owner_plan(key)[0]


def draw_new_owner(key, part):
    return owner_plan(key)[1]


def draw_state(key, part):
    first, second = jax.random.split(jax.random.fold_in(key, 11))
    extent = (6, GROUPS * ELEM_DEV, VOX_SIDE, VOX_PLANE)
    single = (1, GROUPS * ELEM_DEV, VOX_SIDE, VOX_PLANE)
    plastic_part = jnp.clip(0.15 * jax.random.normal(first, extent, jnp.float32), -0.6, 0.6)
    hardening = jax.random.uniform(second, single, jnp.float32, 0.0, 0.5)
    return jnp.concatenate([plastic_part, hardening], axis=0)


def draw_micro_moduli(key, part):
    noise = jax.random.uniform(jax.random.fold_in(key, 13), (4, VOX_SIDE, VOX_PLANE), jnp.float32)
    basis = 0.5 * jnp.exp(noise * jnp.log(4.0))
    ramp = 1.0 + 2.0 * jnp.arange(VOX_SIDE, dtype=jnp.float32) / (VOX_SIDE - 1)
    return basis * ramp[None, :, None]


def with_ends(array, stream_key, least, high):
    shape = array.shape
    place = [jax.random.randint(jax.random.fold_in(stream_key, axis), (), 0, shape[axis]) for axis in range(len(shape))]
    array = array.at[tuple(place)].set(least)
    longest = shape.index(max(shape))
    place[longest] = (place[longest] + 1) % shape[longest]
    return array.at[tuple(place)].set(high)


def steps_of(stream_key, dims, cuts, low, high):
    def one(dim, shards_of):
        heights = jax.random.uniform(jax.random.fold_in(jax.random.fold_in(stream_key, 6), dim), (shards_of,), jnp.float32, low / len(cuts), high / len(cuts))
        return jnp.repeat(jnp.exp(heights), dims[dim] // shards_of).reshape((-1,) + (1,) * (len(dims) - dim - 1))

    factor_of = one(*cuts[0])
    for cut in cuts[1:]:
        factor_of = factor_of * one(*cut)
    return factor_of


def gaussian(own_key, dims, scale, most, cuts=(), kind=jnp.bfloat16):
    array = jax.random.normal(own_key, dims, jnp.float32) * scale
    if len(cuts) > 0:
        array = steps_of(own_key, dims, cuts, -0.22, 0.18) * array
    return jnp.clip(array, min=-most, max=most).astype(kind)


def setup_inputs(seed: int = 0) -> dict:
    key_list = jax.random.split(jax.random.key(seed), 12)
    return {
        "displacement": gaussian(key_list[0], (3, GROUPS * NODE_DEV), 0.2, 1.2, ((1, 16),), jnp.float32),
        "load": gaussian(key_list[1], (3, GROUPS * NODE_DEV), 1.0, 6.0, ((1, 16),), jnp.float32),
        "conn": with_ends(jax.random.randint(key_list[2], (8, GROUPS * ELEM_DEV), 0, NODE_DEV + HALO_NODES), jax.random.fold_in(key_list[2], 1), 0, (NODE_DEV + HALO_NODES) - 1).astype(jnp.int32),
        "halo_list": with_ends(jax.random.randint(key_list[3], (GROUPS * HALO_NODES,), 0, NODE_DEV), jax.random.fold_in(key_list[3], 1), 0, NODE_DEV - 1).astype(jnp.int32),
        "grad_ops": gaussian(key_list[4], (3, 8, GROUPS * ELEM_DEV), 0.5, 3.0, ((2, 16),), jnp.float32),
        "volume": jnp.clip(jnp.exp(math.log(2.0) - 1.3862944 * jax.random.uniform(key_list[5], (GROUPS * ELEM_DEV,), jnp.float32) ** steps_of(key_list[5], (GROUPS * ELEM_DEV,), ((0, 16),), -0.2, 0.2)), 0.5, 2.0),
        "elastic_moduli": jnp.clip(jnp.exp(math.log(4.0) - 1.3862944 * jax.random.uniform(key_list[6], (2, GROUPS * ELEM_DEV), jnp.float32) ** steps_of(key_list[6], (2, GROUPS * ELEM_DEV), ((1, 16),), -0.2, 0.2)), 1.0, 4.0),
        "plastic_mask": draw_plastic_mask(jax.random.fold_in(key_list[11], 71), 0),
        "new_owner": draw_new_owner(jax.random.fold_in(key_list[11], 71), 0),
        "state": draw_state(jax.random.fold_in(key_list[11], 71), 0),
        "micro_moduli": draw_micro_moduli(jax.random.fold_in(key_list[11], 71), 0),
    }


LAM_REF = 3.0
MU_REF = 3.0

def strain_tensor(disp_el, grad_el):
    products = [[lax.optimization_barrier(jnp.sum(disp_el[i] * grad_el[j], axis=0)) for j in range(3)] for i in range(3)]
    return jnp.stack([products[0][0], products[1][1], products[2][2], 0.5 * (products[1][2] + products[2][1]), 0.5 * (products[0][2] + products[2][0]), 0.5 * (products[0][1] + products[1][0])])

def full_tensor(voigt):
    return [[voigt[0], voigt[5], voigt[4]], [voigt[5], voigt[1], voigt[3]], [voigt[4], voigt[3], voigt[2]]]

def nodal_forces(stress, grad_el, volume):
    tensor = full_tensor(stress)
    return jnp.stack([volume * (tensor[i][0] * grad_el[0] + tensor[i][1] * grad_el[1] + tensor[i][2] * grad_el[2]) for i in range(3)])

def elastic_stress(strain, moduli):
    lame_first = moduli[0]
    shear_mod = moduli[1]
    trace = strain[0] + strain[1] + strain[2]
    return jnp.stack([lame_first * trace + 2.0 * shear_mod * strain[c] for c in range(3)] + [2.0 * shear_mod * strain[c] for c in range(3, 6)])

def return_map(strain, state, props):
    lame_first, shear_mod, yield_base, harden = (props[0], props[1], props[2], props[3])
    elastic = [strain[c] - state[c] for c in range(6)]
    trace = elastic[0] + elastic[1] + elastic[2]
    trial = [lame_first * trace + 2.0 * shear_mod * elastic[c] for c in range(3)] + [2.0 * shear_mod * elastic[c] for c in range(3, 6)]
    pressure = (trial[0] + trial[1] + trial[2]) / 3.0
    deviator = [trial[0] - pressure, trial[1] - pressure, trial[2] - pressure, trial[3], trial[4], trial[5]]
    squared = deviator[0] ** 2 + deviator[1] ** 2 + deviator[2] ** 2 + 2.0 * (deviator[3] ** 2 + deviator[4] ** 2 + deviator[5] ** 2)
    equivalent = jnp.sqrt(1.5 * squared)
    strength = yield_base + harden * state[6]
    excess = jnp.maximum(equivalent - strength, 0.0)
    stiffer = 3.0 * shear_mod + harden
    factor = excess / (stiffer * jnp.maximum(equivalent, strength))
    stress = jnp.stack([trial[c] - 3.0 * shear_mod * factor * deviator[c] for c in range(6)])
    new_state = jnp.stack([state[c] + 1.5 * factor * deviator[c] for c in range(6)] + [state[6] + excess / stiffer])
    return (stress, new_state)

def green_apply(tau, freq_x, freq_y, freq_z):
    trac_x = tau[0] * freq_x + tau[5] * freq_y + tau[4] * freq_z
    trac_y = tau[5] * freq_x + tau[1] * freq_y + tau[3] * freq_z
    trac_z = tau[4] * freq_x + tau[3] * freq_y + tau[2] * freq_z
    norm_sq = freq_x * freq_x + freq_y * freq_y + freq_z * freq_z
    inverse = jnp.where(norm_sq > 0, 1.0 / jnp.maximum(norm_sq, 1.0), 0.0)
    coupling = (LAM_REF + MU_REF) / (LAM_REF + 2.0 * MU_REF)
    along = (freq_x * trac_x + freq_y * trac_y + freq_z * trac_z) * inverse
    wave_x = (trac_x - coupling * along * freq_x) * inverse / MU_REF
    wave_y = (trac_y - coupling * along * freq_y) * inverse / MU_REF
    wave_z = (trac_z - coupling * along * freq_z) * inverse / MU_REF
    return [freq_x * wave_x, freq_y * wave_y, freq_z * wave_z, 0.5 * (freq_y * wave_z + freq_z * wave_y), 0.5 * (freq_x * wave_z + freq_z * wave_x), 0.5 * (freq_x * wave_y + freq_y * wave_x)]

def solve_block(states, strains, props):
    index = jnp.arange(VOX_SIDE, dtype=jnp.int32)
    signed = jnp.where(index < VOX_SIDE // 2, index, index - VOX_SIDE).astype(jnp.float32)
    freq_x = signed[:, None, None]
    freq_y = signed[None, :, None]
    freq_z = signed[None, None, :]
    field = jnp.broadcast_to(strains[:, :, None, None, None], (6,) + states.shape[1:])
    for iteration in range(SWEEPS):
        stress, _ = return_map(field, states, props)
        spectrum = jnp.fft.fftn(stress, axes=(2, 3, 4))
        update = jnp.stack(green_apply([spectrum[c] for c in range(6)], freq_x, freq_y, freq_z))
        field = field - jnp.real(jnp.fft.ifftn(update, axes=(2, 3, 4)))
    stress, new_state = return_map(field, states, props)
    return (new_state, lax.optimization_barrier(jnp.mean(stress, axis=(2, 3, 4))))

def reference(displacement, load, conn, halo_list, grad_ops, volume, elastic_moduli, plastic_mask, new_owner, state, micro_moduli):
    points = GROUPS * ELEM_DEV
    point_ids = jnp.arange(points, dtype=jnp.int32)
    group_of = point_ids // ELEM_DEV
    previous = (group_of - 1) % GROUPS
    halo_slot = jnp.clip(conn - NODE_DEV, 0, HALO_NODES - 1)
    halo_node = previous[None, :] * NODE_DEV + halo_list[previous[None, :] * HALO_NODES + halo_slot]
    global_node = jnp.where(conn < NODE_DEV, group_of[None, :] * NODE_DEV + conn, halo_node).astype(jnp.int32)
    disp_el = displacement[:, global_node]
    strain = strain_tensor(disp_el, grad_ops)
    plastic = plastic_mask == 1
    sort_key = jnp.where(plastic, new_owner * points + point_ids, GROUPS * points + point_ids)
    chosen = jnp.argsort(sort_key)[:GROUPS * RECV_AGG].astype(jnp.int32)
    blocks = chosen.reshape(-1, 8)
    cube_moduli = micro_moduli.reshape(4, VOX_SIDE, VOX_SIDE, VOX_SIDE)

    def solve_one(indices):
        states = state[:, indices].reshape(7, 8, VOX_SIDE, VOX_SIDE, VOX_SIDE)
        return solve_block(states, strain[:, indices], cube_moduli)
    new_states, averaged = lax.map(solve_one, blocks)
    moved_state = jnp.transpose(new_states, (1, 0, 2, 3, 4, 5)).reshape(7, GROUPS * RECV_AGG, VOX_SIDE, VOX_PLANE)
    averaged = jnp.transpose(averaged, (1, 0, 2)).reshape(6, GROUPS * RECV_AGG)
    stress = elastic_stress(strain, elastic_moduli).at[:, chosen].set(averaged)
    forces = nodal_forces(stress, grad_ops, volume)
    assembled = jnp.zeros((3, GROUPS * NODE_DEV), jnp.float32).at[:, global_node].add(forces)
    return (assembled - load, moved_state)
```

```python
import functools
import math

import jax
import jax.numpy as jnp
import numpy as np
from jax import lax
from jax.experimental import pallas as pl
from jax.experimental.pallas import tpu as pltpu
from jax.sharding import PartitionSpec as P

RECV_AGG = 24
PLASTIC_MAX = 48
VOX_SIDE = 16
VOX_PLANE = 256
SWEEPS = 4
HALF = VOX_SIDE // 2

LAM_REF = 3.0
MU_REF = 3.0
FULL_PREC = lax.Precision.HIGHEST

ROOT = math.sqrt(0.5)
COS1 = math.cos(math.pi / 8)
COS3 = math.cos(3 * math.pi / 8)
PAIRS = [(i, j) for i in range(6) for j in range(i, 6)]


def shifted(block, axis, distance):
    devices = range(lax.axis_size(axis))
    route = [((i - distance) % len(devices), i) for i in devices]
    return lax.ppermute(block, axis, route)


def gather_vox(block):
    ranks = lax.axis_size("vox")
    pieces = jnp.stack([block] + [shifted(block, "vox", d) for d in range(1, ranks)])
    me = lax.axis_index("vox")
    if ranks == 2:
        return jnp.where(me == 0, pieces, pieces[::-1])
    return pieces[(me - jnp.arange(ranks)) % ranks]


def green_tables():
    line = np.arange(VOX_SIDE)
    signed = np.where(line < HALF, line, line - VOX_SIDE).astype(np.float64)
    freq = np.stack(np.meshgrid(signed, signed, signed, indexing="ij"))
    norm = np.sum(freq * freq, axis=0)
    inverse = np.where(norm > 0, 1.0 / np.maximum(norm, 1.0), 0.0)
    coupling = (LAM_REF + MU_REF) / (LAM_REF + 2.0 * MU_REF)
    spots = [(0, 0), (1, 1), (2, 2), (1, 2), (0, 2), (0, 1)]
    table = np.zeros((6, 6) + norm.shape)
    for j, (a, b) in enumerate(spots):
        tau = np.zeros((3, 3))
        tau[a, b] = tau[b, a] = 1.0
        trac = np.einsum("ij,jxyz->ixyz", tau, freq)
        along = np.sum(freq * trac, axis=0) * inverse
        wave = (trac - coupling * along * freq) * inverse / MU_REF
        for i, (c, d) in enumerate(spots):
            table[i, j] = 0.5 * (freq[c] * wave[d] + freq[d] * wave[c])
    back = -line % VOX_SIDE
    flipped = table[:, :, back][:, :, :, back][:, :, :, :, back]
    even = 0.5 * (table + flipped) / VOX_SIDE**3
    even[:, 3:] *= 0.5
    stacked = np.stack([even[i, j] for i, j in PAIRS])
    return stacked.reshape(len(PAIRS), VOX_SIDE, VOX_PLANE).astype(np.float32)


def plane_tables():
    plane = np.arange(VOX_PLANE)
    rows, cols = plane // VOX_SIDE, plane % VOX_SIDE
    phase = (rows[:, None] * rows[None, :] + cols[:, None] * cols[None, :]) % VOX_SIDE
    angle = phase * (2.0 * math.pi / VOX_SIDE)
    plus = jnp.asarray((np.cos(angle) + np.sin(angle)).astype(np.float32))
    minus = jnp.asarray((np.cos(angle) - np.sin(angle)).astype(np.float32))
    out = []
    for table in (plus, minus):
        high = table.astype(jnp.bfloat16)
        out += [high, (table - high.astype(jnp.float32)).astype(jnp.bfloat16)]
    return jnp.stack(out)


def cosine_line(a):
    sums = [None] + [a[x] + a[8 - x] for x in (1, 2, 3)]
    diffs = [None] + [a[x] - a[8 - x] for x in (1, 2, 3)]
    even0, odd0 = a[0] + a[8], a[0] - a[8]
    outer, inner = even0 + a[4], even0 - a[4]
    spread = sums[1] + sums[3]
    slant = ROOT * (sums[1] - sums[3])
    mid = ROOT * diffs[2]
    first = COS1 * diffs[1] + COS3 * diffs[3]
    second = COS3 * diffs[1] - COS1 * diffs[3]
    top, low = odd0 + mid, odd0 - mid
    core = outer + sums[2]
    return [
        core + spread,
        top + first,
        inner + slant,
        low + second,
        outer - sums[2],
        low - second,
        inner - slant,
        top - first,
        core - spread,
    ]


def sine_line(b):
    sums = [None] + [b[x] + b[8 - x] for x in (1, 2, 3)]
    diffs = [None] + [b[x] - b[8 - x] for x in (1, 2, 3)]
    slant = ROOT * (diffs[1] + diffs[3])
    mid = ROOT * sums[2]
    first = COS3 * sums[1] + COS1 * sums[3]
    second = COS1 * sums[1] - COS3 * sums[3]
    return [
        None,
        (first + mid) + b[4],
        slant + diffs[2],
        (second + mid) - b[4],
        diffs[1] - diffs[3],
        (second - mid) + b[4],
        slant - diffs[2],
        (first - mid) - b[4],
    ]


def split_dot(block, table_ref, first):
    high = block.astype(jnp.bfloat16)
    low = (block - high.astype(jnp.float32)).astype(jnp.bfloat16)
    dot = functools.partial(jnp.dot, preferred_element_type=jnp.float32)
    return dot(high, table_ref[first]) + (dot(high, table_ref[first + 1]) + dot(low, table_ref[first]))


def voxel_law(strain, state_ref, props_ref, x):
    row = pl.ds(x, 1)
    lam, mu = props_ref[0, row, :], props_ref[1, row, :]
    yield_base, harden = props_ref[2, row, :], props_ref[3, row, :]
    two_mu, three_mu = 2.0 * mu, 3.0 * mu
    stiff_inv = 1.0 / (three_mu + harden)
    bulk = lam + two_mu * (1.0 / 3.0)
    elastic = [strain[c] - state_ref[c, x] for c in range(6)]
    trace = elastic[0] + elastic[1] + elastic[2]
    third = trace * (1.0 / 3.0)
    shape = [elastic[c] - third for c in range(3)] + elastic[3:]
    normal = shape[0] * shape[0] + shape[1] * shape[1] + shape[2] * shape[2]
    shear = shape[3] * shape[3] + shape[4] * shape[4] + shape[5] * shape[5]
    equivalent = two_mu * jnp.sqrt(1.5 * (normal + 2.0 * shear))
    strength = yield_base + harden * state_ref[6, x]
    gain = jnp.maximum(equivalent - strength, 0.0) * stiff_inv
    factor = gain / jnp.maximum(equivalent, strength)
    keep = two_mu * (1.0 - three_mu * factor)
    pressure = bulk * trace
    stress = [pressure + keep * shape[c] for c in range(3)] + [keep * shape[c] for c in range(3, 6)]
    return stress, shape, (1.5 * two_mu) * factor, gain


def solve_kernel(strain_ref, valid_ref, state_ref, props_ref, green_ref, plane_ref, new_ref, mean_ref, eps, work, cos_ref, sin_ref):
    rows = state_ref.shape[2]
    for c in range(6):
        start = jnp.broadcast_to(strain_ref[c], (VOX_SIDE, rows, VOX_PLANE))
        eps[c] = start

    def sweep(step, carry):
        def law(x, inner):
            stress, _, _, _ = voxel_law([eps[c, x] for c in range(6)], state_ref, props_ref, x)
            for c in range(6):
                work[c, x] = stress[c]
            return inner

        lax.fori_loop(0, VOX_SIDE, law, 0)

        def forward(c, inner):
            field = [work[c, x] for x in range(VOX_SIDE)]
            sums = [field[0]] + [field[x] + field[VOX_SIDE - x] for x in range(1, HALF)] + [field[HALF]]
            diffs = [None] + [field[x] - field[VOX_SIDE - x] for x in range(1, HALF)]
            for k, value in enumerate(cosine_line(sums)):
                cos_ref[c, k] = value
            for k, value in enumerate(sine_line(diffs)):
                if k > 0:
                    sin_ref[c, k - 1] = value
            return inner

        lax.fori_loop(0, 6, forward, 0)

        def plane():
            for ref, first in ((cos_ref, 0), (sin_ref, 2)):
                flat = ref[...].reshape(6 * ref.shape[1] * rows, VOX_PLANE)
                ref[...] = split_dot(flat, plane_ref, first).reshape(ref.shape)

        def apply(field, k):
            row = pl.ds(k, 1)
            field = field[:3] + [2.0 * field[c] for c in range(3, 6)]
            total = [None] * 6
            for n, (i, j) in enumerate(PAIRS):
                entry = green_ref[n, row, :]
                for a, b in [(i, j), (j, i)][: 1 + (i != j)]:
                    term = entry * field[b]
                    total[a] = term if total[a] is None else total[a] + term
            return total

        plane()
        for k in (0, HALF):
            result = apply([cos_ref[c, k] for c in range(6)], k)
            for c in range(6):
                cos_ref[c, k] = result[c]

        def mix(k, inner):
            even = [cos_ref[c, k] for c in range(6)]
            odd = [sin_ref[c, k - 1] for c in range(6)]
            ahead = apply([even[c] + odd[c] for c in range(6)], k)
            behind = apply([even[c] - odd[c] for c in range(6)], VOX_SIDE - k)
            for c in range(6):
                cos_ref[c, k] = ahead[c] + behind[c]
                sin_ref[c, k - 1] = ahead[c] - behind[c]
            return inner

        lax.fori_loop(1, HALF, mix, 0)
        plane()

        def backward(c, inner):
            even = cosine_line([cos_ref[c, k] for k in range(HALF + 1)])
            odd = sine_line([None] + [sin_ref[c, k - 1] for k in range(1, HALF)])
            eps[c, 0] = eps[c, 0] - even[0]
            eps[c, HALF] = eps[c, HALF] - even[HALF]
            for x in range(1, HALF):
                eps[c, x] = eps[c, x] - (even[x] + odd[x])
                eps[c, VOX_SIDE - x] = eps[c, VOX_SIDE - x] - (even[x] - odd[x])
            return inner

        lax.fori_loop(0, 6, backward, 0)
        return carry

    lax.fori_loop(0, SWEEPS, sweep, 0)
    valid = valid_ref[...] > 0.5

    def finish(x, totals):
        stress, shape, scale, gain = voxel_law([eps[c, x] for c in range(6)], state_ref, props_ref, x)
        for c in range(6):
            new_ref[c, x] = state_ref[c, x] + scale * shape[c]
        new_ref[6, x] = jnp.where(valid, state_ref[6, x] + gain, -1.0)
        return tuple(totals[c] + stress[c] for c in range(6))

    zero = jnp.zeros((rows, VOX_PLANE), jnp.float32)
    totals = lax.fori_loop(0, VOX_SIDE, finish, (zero,) * 6)
    for c in range(6):
        total = jnp.sum(totals[c], axis=1, keepdims=True) / VOX_SIDE**3
        mean_ref[c] = jnp.broadcast_to(total, mean_ref.shape[1:])


def micro_solve(states, strains, valid, moduli, tables):
    rows = states.shape[2]
    strain_rows = jnp.broadcast_to(strains[:, :, None], (6, rows, VOX_PLANE))
    valid_rows = jnp.broadcast_to(valid[:, None], (rows, VOX_PLANE))
    vmem = pl.BlockSpec(memory_space=pltpu.VMEM)
    cells = VOX_SIDE * rows * VOX_PLANE
    updated, mean = pl.pallas_call(
        solve_kernel,
        out_shape=(
            jax.ShapeDtypeStruct(states.shape, jnp.float32),
            jax.ShapeDtypeStruct((6, rows, 128), jnp.float32),
        ),
        in_specs=[vmem] * 6,
        out_specs=(vmem, vmem),
        scratch_shapes=[
            pltpu.VMEM((6, VOX_SIDE, rows, VOX_PLANE), jnp.float32),
            pltpu.VMEM((6, VOX_SIDE, rows, VOX_PLANE), jnp.float32),
            pltpu.VMEM((6, HALF + 1, rows, VOX_PLANE), jnp.float32),
            pltpu.VMEM((6, HALF - 1, rows, VOX_PLANE), jnp.float32),
        ],
        compiler_params=pltpu.CompilerParams(vmem_limit_bytes=24 * 2**20),
        cost_estimate=pl.CostEstimate(
            flops=SWEEPS * 2 * 3 * 2 * 6 * cells * VOX_PLANE,
            bytes_accessed=2 * 7 * cells * 4,
            transcendentals=SWEEPS * cells,
        ),
    )(strain_rows, valid_rows, states, moduli, *tables)
    return updated, mean[:, :, 0]


def strain_tensor(disp_el, grad_el):
    products = [[jnp.sum(disp_el[i] * grad_el[j], axis=0) for j in range(3)] for i in range(3)]
    return jnp.stack(
        [
            products[0][0],
            products[1][1],
            products[2][2],
            0.5 * (products[1][2] + products[2][1]),
            0.5 * (products[0][2] + products[2][0]),
            0.5 * (products[0][1] + products[1][0]),
        ]
    )


def full_tensor(voigt):
    return [
        [voigt[0], voigt[5], voigt[4]],
        [voigt[5], voigt[1], voigt[3]],
        [voigt[4], voigt[3], voigt[2]],
    ]


def nodal_forces(stress, grad_el, volume):
    tensor = full_tensor(stress)
    return jnp.stack(
        [
            volume
            * (tensor[i][0] * grad_el[0] + tensor[i][1] * grad_el[1] + tensor[i][2] * grad_el[2])
            for i in range(3)
        ]
    )


def elastic_stress(strain, moduli):
    lame_first = moduli[0]
    shear_mod = moduli[1]
    trace = strain[0] + strain[1] + strain[2]
    return jnp.stack(
        [lame_first * trace + 2.0 * shear_mod * strain[c] for c in range(3)]
        + [2.0 * shear_mod * strain[c] for c in range(3, 6)]
    )


def local(
    displacement,
    load,
    conn,
    halo_list,
    grad_ops,
    volume,
    elastic_moduli,
    plastic_mask,
    new_owner,
    state,
    micro_moduli,
):
    groups = lax.axis_size("macro")
    ranks = lax.axis_size("vox")
    me = lax.axis_index("vox")
    own_nodes = displacement.shape[1]
    elements = conn.shape[1]
    thickness = state.shape[2]
    per_rank = groups // ranks
    tables = (jnp.asarray(green_tables()), plane_tables())
    moduli = jnp.transpose(gather_vox(micro_moduli), (1, 0, 2, 3)).reshape(4, VOX_SIDE, VOX_PLANE)
    node_ids = jnp.arange(own_nodes, dtype=jnp.int32)
    halo_match = (halo_list[:, None] == node_ids[None, :]).astype(jnp.float32)
    halo_out = jnp.dot(displacement, halo_match.T, precision=FULL_PREC)
    halo_disp = shifted(halo_out, "macro", 1)
    local_disp = jnp.concatenate([displacement, halo_disp], axis=1)
    all_ids = jnp.arange(local_disp.shape[1], dtype=jnp.int32)
    node_match = (conn[:, :, None] == all_ids[None, None, :]).astype(jnp.float32)
    disp_el = jnp.einsum("in,aen->iae", local_disp, node_match, precision=FULL_PREC)
    strain = strain_tensor(disp_el, grad_ops)
    plastic = plastic_mask == 1
    point_ids = jnp.arange(elements, dtype=jnp.int32)
    same_owner = (
        (new_owner[:, None] == new_owner[None, :])
        & plastic[:, None]
        & plastic[None, :]
        & (point_ids[None, :] < point_ids[:, None])
    )
    owner_rank = jnp.sum(same_owner.astype(jnp.int32), axis=1)
    capacity = (PLASTIC_MAX + groups - 1) // groups
    send_slot = jnp.where(plastic, owner_rank * groups + new_owner, -1)
    slot_ids = jnp.arange(groups * capacity, dtype=jnp.int32)
    slot_match = slot_ids[:, None] == send_slot[None, :]
    match_float = slot_match.astype(jnp.float32)
    slot_valid = jnp.sum(match_float, axis=1)
    slot_source = jnp.sum(jnp.where(slot_match, point_ids[None, :], 0), axis=1)
    slot_strain = jnp.dot(strain, match_float.T, precision=FULL_PREC)
    moved, means = [], []
    for chunk in range(capacity):
        base = chunk * groups
        picked = state[:, slot_source[base : base + groups]]
        picked = picked.reshape(7, ranks, per_rank, thickness, VOX_PLANE)
        picked = jnp.swapaxes(picked, 2, 3)
        whole = lax.all_to_all(picked, "vox", split_axis=1, concat_axis=1, tiled=True)
        whole = whole.reshape(7, VOX_SIDE, per_rank, VOX_PLANE)
        mine = base + me * per_rank
        updated, mean = micro_solve(
            whole,
            lax.dynamic_slice_in_dim(slot_strain, mine, per_rank, 1),
            lax.dynamic_slice_in_dim(slot_valid, mine, per_rank, 0),
            moduli,
            tables,
        )
        means.append(mean)
        slabs = updated.reshape(7, ranks, thickness, per_rank, VOX_PLANE)
        slabs = lax.all_to_all(slabs, "vox", split_axis=1, concat_axis=1, tiled=True)
        slabs = jnp.swapaxes(slabs, 2, 3).reshape(7, groups, thickness, VOX_PLANE)
        moved.append(lax.all_to_all(slabs, "macro", split_axis=1, concat_axis=1, tiled=True))
    averaged = jnp.moveaxis(gather_vox(jnp.stack(means, axis=1)), 0, 2)
    averaged = averaged.reshape(6, capacity * groups)
    stress_plastic = jnp.dot(averaged, match_float, precision=FULL_PREC)
    stress = jnp.where(plastic[None, :], stress_plastic, elastic_stress(strain, elastic_moduli))
    forces = nodal_forces(stress, grad_ops, volume)
    assembled = jnp.einsum("iae,aen->in", forces, node_match, precision=FULL_PREC)
    returned_force = shifted(assembled[:, own_nodes:], "macro", -1)
    residual = (
        assembled[:, :own_nodes] + jnp.dot(returned_force, halo_match, precision=FULL_PREC) - load
    )
    arrived = jnp.concatenate(moved, axis=1)
    full = jnp.stack([block[6, :, 0, 0] >= 0.0 for block in moved], axis=1).reshape(-1)
    position = jnp.cumsum(full.astype(jnp.int32)) - 1
    wanted = jnp.arange(RECV_AGG, dtype=jnp.int32)
    places = jnp.arange(groups * capacity, dtype=jnp.int32)
    places = (places % capacity) * groups + places // capacity
    chosen = jnp.sum(
        jnp.where((wanted[:, None] == position[None, :]) & full[None, :], places[None, :], 0), axis=1
    )
    return (residual, arrived[:, chosen])


def solution(mesh):
    return jax.shard_map(
        local,
        mesh=mesh,
        in_specs=(
            P(None, "macro"),
            P(None, "macro"),
            P(None, "macro"),
            P("macro"),
            P(None, None, "macro"),
            P("macro"),
            P(None, "macro"),
            P("macro"),
            P("macro"),
            P(None, "macro", "vox", None),
            P(None, "vox", None),
        ),
        out_specs=(P(None, "macro"), P(None, "macro", "vox", None)),
        check_vma=False,
    )
```

```python
import functools
import math

import jax
import jax.numpy as jnp
import numpy as np
from jax import lax
from jax.experimental import pallas as pl
from jax.experimental.pallas import tpu as pltpu
from jax.sharding import PartitionSpec as P

RECV_AGG = 24
PLASTIC_MAX = 48
VOX_SIDE = 16
VOX_PLANE = 256
SWEEPS = 4
HALF = VOX_SIDE // 2

LAM_REF = 3.0
MU_REF = 3.0
FULL_PREC = lax.Precision.HIGHEST

ROOT = math.sqrt(0.5)
COS1 = math.cos(math.pi / 8)
COS3 = math.cos(3 * math.pi / 8)
PAIRS = [(i, j) for i in range(6) for j in range(i, 6)]


def shifted(block, axis, distance):
    devices = range(lax.axis_size(axis))
    route = [((i - distance) % len(devices), i) for i in devices]
    return lax.ppermute(block, axis, route)


def by_rank(pieces, axis):
    ranks = len(pieces)
    me = lax.axis_index("vox")
    if ranks == 2:
        straight = jnp.concatenate(pieces, axis=axis)
        return jnp.where(me == 0, straight, jnp.concatenate(pieces[::-1], axis=axis))
    order = (me - jnp.arange(ranks)) % ranks
    stacked = jnp.moveaxis(jnp.stack(pieces)[order], 0, axis)
    shape = list(pieces[0].shape)
    shape[axis] *= ranks
    return stacked.reshape(shape)


def green_tables():
    line = np.arange(VOX_SIDE)
    signed = np.where(line < HALF, line, line - VOX_SIDE).astype(np.float64)
    freq = np.stack(np.meshgrid(signed, signed, signed, indexing="ij"))
    norm = np.sum(freq * freq, axis=0)
    inverse = np.where(norm > 0, 1.0 / np.maximum(norm, 1.0), 0.0)
    coupling = (LAM_REF + MU_REF) / (LAM_REF + 2.0 * MU_REF)
    spots = [(0, 0), (1, 1), (2, 2), (1, 2), (0, 2), (0, 1)]
    table = np.zeros((6, 6) + norm.shape)
    for j, (a, b) in enumerate(spots):
        tau = np.zeros((3, 3))
        tau[a, b] = tau[b, a] = 1.0
        trac = np.einsum("ij,jxyz->ixyz", tau, freq)
        along = np.sum(freq * trac, axis=0) * inverse
        wave = (trac - coupling * along * freq) * inverse / MU_REF
        for i, (c, d) in enumerate(spots):
            table[i, j] = 0.5 * (freq[c] * wave[d] + freq[d] * wave[c])
    back = -line % VOX_SIDE
    flipped = table[:, :, back][:, :, :, back][:, :, :, :, back]
    even = 0.5 * (table + flipped) / VOX_SIDE**3
    even[:, 3:] *= 0.5
    stacked = np.stack([even[i, j] for i, j in PAIRS])
    return stacked.reshape(len(PAIRS), VOX_SIDE, VOX_PLANE).astype(np.float32)


def plane_tables():
    plane = np.arange(VOX_PLANE)
    rows, cols = plane // VOX_SIDE, plane % VOX_SIDE
    phase = (rows[:, None] * rows[None, :] + cols[:, None] * cols[None, :]) % VOX_SIDE
    angle = phase * (2.0 * math.pi / VOX_SIDE)
    plus = jnp.asarray((np.cos(angle) + np.sin(angle)).astype(np.float32))
    minus = jnp.asarray((np.cos(angle) - np.sin(angle)).astype(np.float32))
    out = []
    for table in (plus, minus):
        high = table.astype(jnp.bfloat16)
        out += [high, (table - high.astype(jnp.float32)).astype(jnp.bfloat16)]
    return jnp.stack(out)


def cosine_line(a):
    sums = [None] + [a[x] + a[8 - x] for x in (1, 2, 3)]
    diffs = [None] + [a[x] - a[8 - x] for x in (1, 2, 3)]
    even0, odd0 = a[0] + a[8], a[0] - a[8]
    outer, inner = even0 + a[4], even0 - a[4]
    spread = sums[1] + sums[3]
    slant = ROOT * (sums[1] - sums[3])
    mid = ROOT * diffs[2]
    first = COS1 * diffs[1] + COS3 * diffs[3]
    second = COS3 * diffs[1] - COS1 * diffs[3]
    top, low = odd0 + mid, odd0 - mid
    core = outer + sums[2]
    return [
        core + spread,
        top + first,
        inner + slant,
        low + second,
        outer - sums[2],
        low - second,
        inner - slant,
        top - first,
        core - spread,
    ]


def sine_line(b):
    sums = [None] + [b[x] + b[8 - x] for x in (1, 2, 3)]
    diffs = [None] + [b[x] - b[8 - x] for x in (1, 2, 3)]
    slant = ROOT * (diffs[1] + diffs[3])
    mid = ROOT * sums[2]
    first = COS3 * sums[1] + COS1 * sums[3]
    second = COS1 * sums[1] - COS3 * sums[3]
    return [
        None,
        (first + mid) + b[4],
        slant + diffs[2],
        (second + mid) - b[4],
        diffs[1] - diffs[3],
        (second - mid) + b[4],
        slant - diffs[2],
        (first - mid) - b[4],
    ]


def split_dot(block, table_ref, first):
    high = block.astype(jnp.bfloat16)
    low = (block - high.astype(jnp.float32)).astype(jnp.bfloat16)
    dot = functools.partial(jnp.dot, preferred_element_type=jnp.float32)
    return dot(high, table_ref[first]) + (dot(high, table_ref[first + 1]) + dot(low, table_ref[first]))


def voxel_law(strain, state_ref, props_ref, place, x):
    row = pl.ds(x, 1)
    lam, mu = props_ref[0, row, :], props_ref[1, row, :]
    yield_base, harden = props_ref[2, row, :], props_ref[3, row, :]
    two_mu, three_mu = 2.0 * mu, 3.0 * mu
    stiff_inv = 1.0 / (three_mu + harden)
    bulk = lam + two_mu * (1.0 / 3.0)
    elastic = [strain[c] - state_ref[c, place] for c in range(6)]
    trace = elastic[0] + elastic[1] + elastic[2]
    third = trace * (1.0 / 3.0)
    shape = [elastic[c] - third for c in range(3)] + elastic[3:]
    normal = shape[0] * shape[0] + shape[1] * shape[1] + shape[2] * shape[2]
    shear = shape[3] * shape[3] + shape[4] * shape[4] + shape[5] * shape[5]
    equivalent = two_mu * jnp.sqrt(1.5 * (normal + 2.0 * shear))
    strength = yield_base + harden * state_ref[6, place]
    gain = jnp.maximum(equivalent - strength, 0.0) * stiff_inv
    factor = gain / jnp.maximum(equivalent, strength)
    keep = two_mu * (1.0 - three_mu * factor)
    pressure = bulk * trace
    stress = [pressure + keep * shape[c] for c in range(3)] + [keep * shape[c] for c in range(3, 6)]
    return stress, shape, (1.5 * two_mu) * factor, gain


def solve_kernel(ranks, strain_ref, valid_ref, props_ref, green_ref, plane_ref, *refs):
    state_refs, new_refs = refs[:ranks], refs[ranks : 2 * ranks]
    mean_ref, eps, work, cos_ref, sin_ref = refs[2 * ranks :]
    thickness, rows = state_refs[0].shape[1:3]
    for c in range(6):
        start = jnp.broadcast_to(strain_ref[c], (VOX_SIDE, rows, VOX_PLANE))
        eps[c] = start

    def sweep(step, carry):
        for slab, state_ref in enumerate(state_refs):

            def law(place, inner, slab=slab, state_ref=state_ref):
                x = slab * thickness + place
                strain = [eps[c, x] for c in range(6)]
                stress = voxel_law(strain, state_ref, props_ref, place, x)[0]
                for c in range(6):
                    work[c, x] = stress[c]
                return inner

            lax.fori_loop(0, thickness, law, 0)

        def forward(c, inner):
            field = [work[c, x] for x in range(VOX_SIDE)]
            sums = [field[0]] + [field[x] + field[VOX_SIDE - x] for x in range(1, HALF)] + [field[HALF]]
            diffs = [None] + [field[x] - field[VOX_SIDE - x] for x in range(1, HALF)]
            for k, value in enumerate(cosine_line(sums)):
                cos_ref[c, k] = value
            for k, value in enumerate(sine_line(diffs)):
                if k > 0:
                    sin_ref[c, k - 1] = value
            return inner

        lax.fori_loop(0, 6, forward, 0)

        def plane():
            for ref, first in ((cos_ref, 0), (sin_ref, 2)):
                flat = ref[...].reshape(6 * ref.shape[1] * rows, VOX_PLANE)
                ref[...] = split_dot(flat, plane_ref, first).reshape(ref.shape)

        def apply(field, k):
            row = pl.ds(k, 1)
            field = field[:3] + [2.0 * field[c] for c in range(3, 6)]
            total = [None] * 6
            for n, (i, j) in enumerate(PAIRS):
                entry = green_ref[n, row, :]
                for a, b in [(i, j), (j, i)][: 1 + (i != j)]:
                    term = entry * field[b]
                    total[a] = term if total[a] is None else total[a] + term
            return total

        plane()
        for k in (0, HALF):
            result = apply([cos_ref[c, k] for c in range(6)], k)
            for c in range(6):
                cos_ref[c, k] = result[c]

        def mix(k, inner):
            even = [cos_ref[c, k] for c in range(6)]
            odd = [sin_ref[c, k - 1] for c in range(6)]
            ahead = apply([even[c] + odd[c] for c in range(6)], k)
            behind = apply([even[c] - odd[c] for c in range(6)], VOX_SIDE - k)
            for c in range(6):
                cos_ref[c, k] = ahead[c] + behind[c]
                sin_ref[c, k - 1] = ahead[c] - behind[c]
            return inner

        lax.fori_loop(1, HALF, mix, 0)
        plane()

        def backward(c, inner):
            even = cosine_line([cos_ref[c, k] for k in range(HALF + 1)])
            odd = sine_line([None] + [sin_ref[c, k - 1] for k in range(1, HALF)])
            eps[c, 0] = eps[c, 0] - even[0]
            eps[c, HALF] = eps[c, HALF] - even[HALF]
            for x in range(1, HALF):
                eps[c, x] = eps[c, x] - (even[x] + odd[x])
                eps[c, VOX_SIDE - x] = eps[c, VOX_SIDE - x] - (even[x] - odd[x])
            return inner

        lax.fori_loop(0, 6, backward, 0)
        return carry

    lax.fori_loop(0, SWEEPS, sweep, 0)
    valid = valid_ref[...] > 0.5

    zero = jnp.zeros((rows, VOX_PLANE), jnp.float32)
    totals = (zero,) * 6
    for slab, (state_ref, new_ref) in enumerate(zip(state_refs, new_refs)):

        def finish(place, totals, slab=slab, state_ref=state_ref, new_ref=new_ref):
            x = slab * thickness + place
            strain = [eps[c, x] for c in range(6)]
            stress, shape, scale, gain = voxel_law(strain, state_ref, props_ref, place, x)
            for c in range(6):
                new_ref[c, place] = state_ref[c, place] + scale * shape[c]
            new_ref[6, place] = jnp.where(valid, state_ref[6, place] + gain, -1.0)
            return tuple(totals[c] + stress[c] for c in range(6))

        totals = lax.fori_loop(0, thickness, finish, totals)
    for c in range(6):
        total = jnp.sum(totals[c], axis=1, keepdims=True) / VOX_SIDE**3
        mean_ref[c] = jnp.broadcast_to(total, mean_ref.shape[1:])


def micro_solve(pieces, strains, valid, moduli, tables):
    ranks = len(pieces)
    rows = pieces[0].shape[2]
    strain_rows = jnp.broadcast_to(strains[:, :, None], (6, rows, VOX_PLANE))
    valid_rows = jnp.broadcast_to(valid[:, None], (rows, VOX_PLANE))
    vmem = pl.BlockSpec(memory_space=pltpu.VMEM)
    cells = VOX_SIDE * rows * VOX_PLANE
    results = pl.pallas_call(
        functools.partial(solve_kernel, ranks),
        out_shape=[jax.ShapeDtypeStruct(pieces[0].shape, jnp.float32)] * ranks
        + [jax.ShapeDtypeStruct((6, rows, 128), jnp.float32)],
        in_specs=[vmem] * (5 + ranks),
        out_specs=[vmem] * (ranks + 1),
        scratch_shapes=[
            pltpu.VMEM((6, VOX_SIDE, rows, VOX_PLANE), jnp.float32),
            pltpu.VMEM((6, VOX_SIDE, rows, VOX_PLANE), jnp.float32),
            pltpu.VMEM((6, HALF + 1, rows, VOX_PLANE), jnp.float32),
            pltpu.VMEM((6, HALF - 1, rows, VOX_PLANE), jnp.float32),
        ],
        compiler_params=pltpu.CompilerParams(vmem_limit_bytes=24 * 2**20),
        cost_estimate=pl.CostEstimate(
            flops=SWEEPS * 2 * 3 * 2 * 6 * cells * VOX_PLANE,
            bytes_accessed=2 * 7 * cells * 4,
            transcendentals=SWEEPS * cells,
        ),
    )(strain_rows, valid_rows, moduli, *tables, *pieces)
    return results[:ranks], results[ranks][:, :, 0]


def strain_tensor(disp_el, grad_el):
    products = [[jnp.sum(disp_el[i] * grad_el[j], axis=0) for j in range(3)] for i in range(3)]
    return jnp.stack(
        [
            products[0][0],
            products[1][1],
            products[2][2],
            0.5 * (products[1][2] + products[2][1]),
            0.5 * (products[0][2] + products[2][0]),
            0.5 * (products[0][1] + products[1][0]),
        ]
    )


def full_tensor(voigt):
    return [
        [voigt[0], voigt[5], voigt[4]],
        [voigt[5], voigt[1], voigt[3]],
        [voigt[4], voigt[3], voigt[2]],
    ]


def nodal_forces(stress, grad_el, volume):
    tensor = full_tensor(stress)
    return jnp.stack(
        [
            volume
            * (tensor[i][0] * grad_el[0] + tensor[i][1] * grad_el[1] + tensor[i][2] * grad_el[2])
            for i in range(3)
        ]
    )


def elastic_stress(strain, moduli):
    lame_first = moduli[0]
    shear_mod = moduli[1]
    trace = strain[0] + strain[1] + strain[2]
    return jnp.stack(
        [lame_first * trace + 2.0 * shear_mod * strain[c] for c in range(3)]
        + [2.0 * shear_mod * strain[c] for c in range(3, 6)]
    )


def local(
    displacement,
    load,
    conn,
    halo_list,
    grad_ops,
    volume,
    elastic_moduli,
    plastic_mask,
    new_owner,
    state,
    micro_moduli,
):
    groups = lax.axis_size("macro")
    ranks = lax.axis_size("vox")
    me = lax.axis_index("vox")
    own_nodes = displacement.shape[1]
    elements = conn.shape[1]
    thickness = state.shape[2]
    per_rank = groups // ranks
    tables = (jnp.asarray(green_tables()), plane_tables())
    moduli = jnp.concatenate(
        [micro_moduli] + [shifted(micro_moduli, "vox", -d) for d in range(1, ranks)], axis=1
    )
    node_ids = jnp.arange(own_nodes, dtype=jnp.int32)
    halo_match = (halo_list[:, None] == node_ids[None, :]).astype(jnp.float32)
    halo_out = jnp.dot(displacement, halo_match.T, precision=FULL_PREC)
    halo_disp = shifted(halo_out, "macro", 1)
    local_disp = jnp.concatenate([displacement, halo_disp], axis=1)
    all_ids = jnp.arange(local_disp.shape[1], dtype=jnp.int32)
    node_match = (conn[:, :, None] == all_ids[None, None, :]).astype(jnp.float32)
    disp_el = jnp.einsum("in,aen->iae", local_disp, node_match, precision=FULL_PREC)
    strain = strain_tensor(disp_el, grad_ops)
    plastic = plastic_mask == 1
    point_ids = jnp.arange(elements, dtype=jnp.int32)
    same_owner = (
        (new_owner[:, None] == new_owner[None, :])
        & plastic[:, None]
        & plastic[None, :]
        & (point_ids[None, :] < point_ids[:, None])
    )
    owner_rank = jnp.sum(same_owner.astype(jnp.int32), axis=1)
    capacity = (PLASTIC_MAX + groups - 1) // groups
    send_slot = jnp.where(plastic, owner_rank * groups + new_owner, -1)
    slot_ids = jnp.arange(groups * capacity, dtype=jnp.int32)
    slot_match = slot_ids[:, None] == send_slot[None, :]
    match_float = slot_match.astype(jnp.float32)
    slot_valid = jnp.sum(match_float, axis=1)
    slot_source = jnp.sum(jnp.where(slot_match, point_ids[None, :], 0), axis=1)
    slot_strain = jnp.dot(strain, match_float.T, precision=FULL_PREC)
    moved, means = [], []
    for chunk in range(capacity):
        base = chunk * groups
        pieces = []
        for d in range(ranks):
            solver = base + (me - d) % ranks * per_rank
            sources = lax.dynamic_slice_in_dim(slot_source, solver, per_rank, 0)
            piece = jnp.swapaxes(state[:, sources], 1, 2)
            pieces.append(shifted(piece, "vox", -d) if d else piece)
        mine = base + me * per_rank
        updated, mean = micro_solve(
            pieces,
            lax.dynamic_slice_in_dim(slot_strain, mine, per_rank, 1),
            lax.dynamic_slice_in_dim(slot_valid, mine, per_rank, 0),
            moduli,
            tables,
        )
        means.append(mean)
        slabs = [updated[0]] + [shifted(updated[d], "vox", d) for d in range(1, ranks)]
        slabs = jnp.swapaxes(by_rank(slabs, 2), 1, 2)
        moved.append(lax.all_to_all(slabs, "macro", split_axis=1, concat_axis=1, tiled=True))
    own_mean = jnp.stack(means, axis=1)
    parts = [own_mean] + [shifted(own_mean, "vox", d) for d in range(1, ranks)]
    averaged = by_rank(parts, 2).reshape(6, capacity * groups)
    stress_plastic = jnp.dot(averaged, match_float, precision=FULL_PREC)
    stress = jnp.where(plastic[None, :], stress_plastic, elastic_stress(strain, elastic_moduli))
    forces = nodal_forces(stress, grad_ops, volume)
    assembled = jnp.einsum("iae,aen->in", forces, node_match, precision=FULL_PREC)
    returned_force = shifted(assembled[:, own_nodes:], "macro", -1)
    residual = (
        assembled[:, :own_nodes] + jnp.dot(returned_force, halo_match, precision=FULL_PREC) - load
    )
    arrived = jnp.concatenate(moved, axis=1)
    full = jnp.stack([block[6, :, 0, 0] >= 0.0 for block in moved], axis=1).reshape(-1)
    position = jnp.cumsum(full.astype(jnp.int32)) - 1
    wanted = jnp.arange(RECV_AGG, dtype=jnp.int32)
    places = jnp.arange(groups * capacity, dtype=jnp.int32)
    places = (places % capacity) * groups + places // capacity
    chosen = jnp.sum(
        jnp.where((wanted[:, None] == position[None, :]) & full[None, :], places[None, :], 0), axis=1
    )
    return (residual, arrived[:, chosen])


def solution(mesh):
    return jax.shard_map(
        local,
        mesh=mesh,
        in_specs=(
            P(None, "macro"),
            P(None, "macro"),
            P(None, "macro"),
            P("macro"),
            P(None, None, "macro"),
            P("macro"),
            P(None, "macro"),
            P("macro"),
            P("macro"),
            P(None, "macro", "vox", None),
            P(None, "vox", None),
        ),
        out_specs=(P(None, "macro"), P(None, "macro", "vox", None)),
        check_vma=False,
    )
```

```python
import functools
import math

import jax
import jax.numpy as jnp
import numpy as np
from jax import lax
from jax.experimental import pallas as pl
from jax.experimental.pallas import tpu as pltpu
from jax.sharding import PartitionSpec as P


RECV_AGG = 24
PLASTIC_MAX = 48
VOX_SIDE = 16
VOX_PLANE = 256
SWEEPS = 4
HALF = VOX_SIDE // 2

LAM_REF = 3.0
MU_REF = 3.0
FULL_PREC = lax.Precision.HIGHEST

ROOT = math.sqrt(0.5)
COS1 = math.cos(math.pi / 8)
COS3 = math.cos(3 * math.pi / 8)
PAIRS = [(i, j) for i in range(6) for j in range(i, 6)]


def shifted(block, axis, distance):
    devices = range(lax.axis_size(axis))
    route = [((i - distance) % len(devices), i) for i in devices]
    return lax.ppermute(block, axis, route)


def by_rank(pieces, axis):
    ranks = len(pieces)
    me = lax.axis_index("vox")
    if ranks == 2:
        straight = jnp.concatenate(pieces, axis=axis)
        return jnp.where(me == 0, straight, jnp.concatenate(pieces[::-1], axis=axis))
    order = (me - jnp.arange(ranks)) % ranks
    stacked = jnp.moveaxis(jnp.stack(pieces)[order], 0, axis)
    shape = list(pieces[0].shape)
    shape[axis] *= ranks
    return stacked.reshape(shape)


def green_tables():
    line = np.arange(VOX_SIDE)
    signed = np.where(line < HALF, line, line - VOX_SIDE).astype(np.float64)
    freq = np.stack(np.meshgrid(signed, signed, signed, indexing="ij"))
    norm = np.sum(freq * freq, axis=0)
    inverse = np.where(norm > 0, 1.0 / np.maximum(norm, 1.0), 0.0)
    coupling = (LAM_REF + MU_REF) / (LAM_REF + 2.0 * MU_REF)
    spots = [(0, 0), (1, 1), (2, 2), (1, 2), (0, 2), (0, 1)]
    table = np.zeros((6, 6) + norm.shape)
    for j, (a, b) in enumerate(spots):
        tau = np.zeros((3, 3))
        tau[a, b] = tau[b, a] = 1.0
        trac = np.einsum("ij,jxyz->ixyz", tau, freq)
        along = np.sum(freq * trac, axis=0) * inverse
        wave = (trac - coupling * along * freq) * inverse / MU_REF
        for i, (c, d) in enumerate(spots):
            table[i, j] = 0.5 * (freq[c] * wave[d] + freq[d] * wave[c])
    back = -line % VOX_SIDE
    flipped = table[:, :, back][:, :, :, back][:, :, :, :, back]
    even = 0.5 * (table + flipped) / VOX_SIDE**3
    even[:, 3:] *= 0.5
    stacked = np.stack([even[i, j] for i, j in PAIRS])
    return stacked.reshape(len(PAIRS), VOX_SIDE, VOX_PLANE).astype(np.float32)


def plane_tables():
    plane = np.arange(VOX_PLANE)
    rows, cols = plane // VOX_SIDE, plane % VOX_SIDE
    phase = (rows[:, None] * rows[None, :] + cols[:, None] * cols[None, :]) % VOX_SIDE
    angle = phase * (2.0 * math.pi / VOX_SIDE)
    plus = jnp.asarray((np.cos(angle) + np.sin(angle)).astype(np.float32))
    minus = jnp.asarray((np.cos(angle) - np.sin(angle)).astype(np.float32))
    out = []
    for table in (plus, minus):
        high = table.astype(jnp.bfloat16)
        out += [high, (table - high.astype(jnp.float32)).astype(jnp.bfloat16)]
    return jnp.stack(out)


def cosine_line(a):
    sums = [None] + [a[x] + a[8 - x] for x in (1, 2, 3)]
    diffs = [None] + [a[x] - a[8 - x] for x in (1, 2, 3)]
    even0, odd0 = a[0] + a[8], a[0] - a[8]
    outer, inner = even0 + a[4], even0 - a[4]
    spread = sums[1] + sums[3]
    slant = ROOT * (sums[1] - sums[3])
    mid = ROOT * diffs[2]
    first = COS1 * diffs[1] + COS3 * diffs[3]
    second = COS3 * diffs[1] - COS1 * diffs[3]
    top, low = odd0 + mid, odd0 - mid
    core = outer + sums[2]
    return [
        core + spread,
        top + first,
        inner + slant,
        low + second,
        outer - sums[2],
        low - second,
        inner - slant,
        top - first,
        core - spread,
    ]


def sine_line(b):
    sums = [None] + [b[x] + b[8 - x] for x in (1, 2, 3)]
    diffs = [None] + [b[x] - b[8 - x] for x in (1, 2, 3)]
    slant = ROOT * (diffs[1] + diffs[3])
    mid = ROOT * sums[2]
    first = COS3 * sums[1] + COS1 * sums[3]
    second = COS1 * sums[1] - COS3 * sums[3]
    return [
        None,
        (first + mid) + b[4],
        slant + diffs[2],
        (second + mid) - b[4],
        diffs[1] - diffs[3],
        (second - mid) + b[4],
        slant - diffs[2],
        (first - mid) - b[4],
    ]


def split_dot(block, table_ref, first):
    high = block.astype(jnp.bfloat16)
    low = (block - high.astype(jnp.float32)).astype(jnp.bfloat16)
    dot = functools.partial(jnp.dot, preferred_element_type=jnp.float32)
    return dot(high, table_ref[first]) + (dot(high, table_ref[first + 1]) + dot(low, table_ref[first]))


def voxel_law(strain, state_ref, props_ref, place, x):
    row = pl.ds(x, 1)
    lam, mu = props_ref[0, row, :], props_ref[1, row, :]
    yield_base, harden = props_ref[2, row, :], props_ref[3, row, :]
    two_mu, three_mu = 2.0 * mu, 3.0 * mu
    stiff_inv = 1.0 / (three_mu + harden)
    bulk = lam + two_mu * (1.0 / 3.0)
    elastic = [strain[c] - state_ref[c, place] for c in range(6)]
    trace = elastic[0] + elastic[1] + elastic[2]
    third = trace * (1.0 / 3.0)
    shape = [elastic[c] - third for c in range(3)] + elastic[3:]
    normal = shape[0] * shape[0] + shape[1] * shape[1] + shape[2] * shape[2]
    shear = shape[3] * shape[3] + shape[4] * shape[4] + shape[5] * shape[5]
    equivalent = two_mu * jnp.sqrt(1.5 * (normal + 2.0 * shear))
    strength = yield_base + harden * state_ref[6, place]
    gain = jnp.maximum(equivalent - strength, 0.0) * stiff_inv
    factor = gain / jnp.maximum(equivalent, strength)
    keep = two_mu * (1.0 - three_mu * factor)
    pressure = bulk * trace
    stress = [pressure + keep * shape[c] for c in range(3)] + [keep * shape[c] for c in range(3, 6)]
    return stress, shape, (1.5 * two_mu) * factor, gain


def solve_kernel(ranks, strain_ref, props_ref, green_ref, plane_ref, *refs):
    state_refs, new_refs = refs[:ranks], refs[ranks : 2 * ranks]
    mean_ref, eps, work, cos_ref, sin_ref = refs[2 * ranks :]
    thickness, rows = state_refs[0].shape[1:3]
    for c in range(6):
        start = jnp.broadcast_to(strain_ref[c], (VOX_SIDE, rows, VOX_PLANE))
        eps[c] = start

    def sweep(step, carry):
        for slab, state_ref in enumerate(state_refs):

            def law(place, inner, slab=slab, state_ref=state_ref):
                x = slab * thickness + place
                strain = [eps[c, x] for c in range(6)]
                stress = voxel_law(strain, state_ref, props_ref, place, x)[0]
                for c in range(6):
                    work[c, x] = stress[c]
                return inner

            lax.fori_loop(0, thickness, law, 0)

        def forward(c, inner):
            field = [work[c, x] for x in range(VOX_SIDE)]
            sums = [field[0]] + [field[x] + field[VOX_SIDE - x] for x in range(1, HALF)] + [field[HALF]]
            diffs = [None] + [field[x] - field[VOX_SIDE - x] for x in range(1, HALF)]
            for k, value in enumerate(cosine_line(sums)):
                cos_ref[c, k] = value
            for k, value in enumerate(sine_line(diffs)):
                if k > 0:
                    sin_ref[c, k - 1] = value
            return inner

        lax.fori_loop(0, 6, forward, 0)

        def plane():
            for ref, first in ((cos_ref, 0), (sin_ref, 2)):
                flat = ref[...].reshape(6 * ref.shape[1] * rows, VOX_PLANE)
                ref[...] = split_dot(flat, plane_ref, first).reshape(ref.shape)

        def apply(field, k):
            row = pl.ds(k, 1)
            field = field[:3] + [2.0 * field[c] for c in range(3, 6)]
            total = [None] * 6
            for n, (i, j) in enumerate(PAIRS):
                entry = green_ref[n, row, :]
                for a, b in [(i, j), (j, i)][: 1 + (i != j)]:
                    term = entry * field[b]
                    total[a] = term if total[a] is None else total[a] + term
            return total

        plane()
        for k in (0, HALF):
            result = apply([cos_ref[c, k] for c in range(6)], k)
            for c in range(6):
                cos_ref[c, k] = result[c]

        def mix(k, inner):
            even = [cos_ref[c, k] for c in range(6)]
            odd = [sin_ref[c, k - 1] for c in range(6)]
            ahead = apply([even[c] + odd[c] for c in range(6)], k)
            behind = apply([even[c] - odd[c] for c in range(6)], VOX_SIDE - k)
            for c in range(6):
                cos_ref[c, k] = ahead[c] + behind[c]
                sin_ref[c, k - 1] = ahead[c] - behind[c]
            return inner

        lax.fori_loop(1, HALF, mix, 0)
        plane()

        def backward(c, inner):
            even = cosine_line([cos_ref[c, k] for k in range(HALF + 1)])
            odd = sine_line([None] + [sin_ref[c, k - 1] for k in range(1, HALF)])
            eps[c, 0] = eps[c, 0] - even[0]
            eps[c, HALF] = eps[c, HALF] - even[HALF]
            for x in range(1, HALF):
                eps[c, x] = eps[c, x] - (even[x] + odd[x])
                eps[c, VOX_SIDE - x] = eps[c, VOX_SIDE - x] - (even[x] - odd[x])
            return inner

        lax.fori_loop(0, 6, backward, 0)
        return carry

    lax.fori_loop(0, SWEEPS, sweep, 0)
    zero = jnp.zeros((rows, VOX_PLANE), jnp.float32)
    totals = (zero,) * 6
    for slab, (state_ref, new_ref) in enumerate(zip(state_refs, new_refs)):

        def finish(place, totals, slab=slab, state_ref=state_ref, new_ref=new_ref):
            x = slab * thickness + place
            strain = [eps[c, x] for c in range(6)]
            stress, shape, scale, gain = voxel_law(strain, state_ref, props_ref, place, x)
            for c in range(6):
                new_ref[c, place] = state_ref[c, place] + scale * shape[c]
            new_ref[6, place] = state_ref[6, place] + gain
            return tuple(totals[c] + stress[c] for c in range(6))

        totals = lax.fori_loop(0, thickness, finish, totals)
    for c in range(6):
        total = jnp.sum(totals[c], axis=1, keepdims=True) / VOX_SIDE**3
        mean_ref[c] = jnp.broadcast_to(total, mean_ref.shape[1:])


def micro_solve(pieces, strains, moduli, tables):
    ranks = len(pieces)
    rows = pieces[0].shape[2]
    strain_rows = jnp.broadcast_to(strains[:, :, None], (6, rows, VOX_PLANE))
    vmem = pl.BlockSpec(memory_space=pltpu.VMEM)
    cells = VOX_SIDE * rows * VOX_PLANE
    results = pl.pallas_call(
        functools.partial(solve_kernel, ranks),
        out_shape=[jax.ShapeDtypeStruct(pieces[0].shape, jnp.float32)] * ranks
        + [jax.ShapeDtypeStruct((6, rows, 128), jnp.float32)],
        in_specs=[vmem] * (4 + ranks),
        out_specs=[vmem] * (ranks + 1),
        scratch_shapes=[
            pltpu.VMEM((6, VOX_SIDE, rows, VOX_PLANE), jnp.float32),
            pltpu.VMEM((6, VOX_SIDE, rows, VOX_PLANE), jnp.float32),
            pltpu.VMEM((6, HALF + 1, rows, VOX_PLANE), jnp.float32),
            pltpu.VMEM((6, HALF - 1, rows, VOX_PLANE), jnp.float32),
        ],
        compiler_params=pltpu.CompilerParams(vmem_limit_bytes=24 * 2**20),
        cost_estimate=pl.CostEstimate(
            flops=SWEEPS * 2 * 3 * 2 * 6 * cells * VOX_PLANE,
            bytes_accessed=2 * 7 * cells * 4,
            transcendentals=SWEEPS * cells,
        ),
    )(strain_rows, moduli, *tables, *pieces)
    return results[:ranks], results[ranks][:, :, 0]


def pick_kernel(order_ref, *refs):
    out_ref = refs[-1]

    def place(j, carry):
        low = 0
        for part in refs[:-1]:
            size = part.shape[1]
            spot = order_ref[j] - low

            @pl.when((spot >= 0) & (spot < size))
            def _(part=part, spot=spot):
                out_ref[:, j] = part[:, spot]

            low += size
        return carry

    lax.fori_loop(0, out_ref.shape[1], place, 0)


def pick_rows(order, parts):
    shape = (parts[0].shape[0], order.shape[0]) + parts[0].shape[2:]
    vmem = pl.BlockSpec(memory_space=pltpu.VMEM)
    return pl.pallas_call(
        pick_kernel,
        out_shape=jax.ShapeDtypeStruct(shape, jnp.float32),
        in_specs=[pl.BlockSpec(memory_space=pltpu.SMEM)] + [vmem] * len(parts),
        out_specs=vmem,
        compiler_params=pltpu.CompilerParams(vmem_limit_bytes=16 * 2**20),
    )(order, *parts)


def strain_tensor(disp_el, grad_el):
    products = [[jnp.sum(disp_el[i] * grad_el[j], axis=0) for j in range(3)] for i in range(3)]
    return jnp.stack(
        [
            products[0][0],
            products[1][1],
            products[2][2],
            0.5 * (products[1][2] + products[2][1]),
            0.5 * (products[0][2] + products[2][0]),
            0.5 * (products[0][1] + products[1][0]),
        ]
    )


def full_tensor(voigt):
    return [
        [voigt[0], voigt[5], voigt[4]],
        [voigt[5], voigt[1], voigt[3]],
        [voigt[4], voigt[3], voigt[2]],
    ]


def nodal_forces(stress, grad_el, volume):
    tensor = full_tensor(stress)
    return jnp.stack(
        [
            volume
            * (tensor[i][0] * grad_el[0] + tensor[i][1] * grad_el[1] + tensor[i][2] * grad_el[2])
            for i in range(3)
        ]
    )


def elastic_stress(strain, moduli):
    lame_first = moduli[0]
    shear_mod = moduli[1]
    trace = strain[0] + strain[1] + strain[2]
    return jnp.stack(
        [lame_first * trace + 2.0 * shear_mod * strain[c] for c in range(3)]
        + [2.0 * shear_mod * strain[c] for c in range(3, 6)]
    )


def local(
    displacement,
    load,
    conn,
    halo_list,
    grad_ops,
    volume,
    elastic_moduli,
    plastic_mask,
    new_owner,
    state,
    micro_moduli,
):
    groups = lax.axis_size("macro")
    ranks = lax.axis_size("vox")
    me = lax.axis_index("vox")
    own_nodes = displacement.shape[1]
    elements = conn.shape[1]
    per_rank = groups // ranks
    tables = (jnp.asarray(green_tables()), plane_tables())
    moduli = jnp.concatenate(
        [micro_moduli] + [shifted(micro_moduli, "vox", -d) for d in range(1, ranks)], axis=1
    )
    node_ids = jnp.arange(own_nodes, dtype=jnp.int32)
    halo_match = (halo_list[:, None] == node_ids[None, :]).astype(jnp.float32)
    halo_out = jnp.dot(displacement, halo_match.T, precision=FULL_PREC)
    halo_disp = shifted(halo_out, "macro", 1)
    local_disp = jnp.concatenate([displacement, halo_disp], axis=1)
    all_ids = jnp.arange(local_disp.shape[1], dtype=jnp.int32)
    node_match = (conn[:, :, None] == all_ids[None, None, :]).astype(jnp.float32)
    disp_el = jnp.einsum("in,aen->iae", local_disp, node_match, precision=FULL_PREC)
    strain = strain_tensor(disp_el, grad_ops)
    plastic = plastic_mask == 1
    point_ids = jnp.arange(elements, dtype=jnp.int32)
    same_owner = (
        (new_owner[:, None] == new_owner[None, :])
        & plastic[:, None]
        & plastic[None, :]
        & (point_ids[None, :] < point_ids[:, None])
    )
    owner_rank = jnp.sum(same_owner.astype(jnp.int32), axis=1)
    capacity = (PLASTIC_MAX + groups - 1) // groups
    send_slot = jnp.where(plastic, owner_rank * groups + new_owner, -1)
    slot_ids = jnp.arange(groups * capacity, dtype=jnp.int32)
    slot_match = slot_ids[:, None] == send_slot[None, :]
    match_float = slot_match.astype(jnp.float32)
    slot_valid = jnp.sum(match_float, axis=1)
    slot_source = jnp.sum(jnp.where(slot_match, point_ids[None, :], 0), axis=1)
    slot_strain = jnp.dot(strain, match_float.T, precision=FULL_PREC)
    valid_rows = jnp.swapaxes(slot_valid.reshape(capacity, groups), 0, 1)
    got_valid = lax.all_to_all(valid_rows, "macro", split_axis=0, concat_axis=0, tiled=True)
    full = got_valid.reshape(-1) > 0.5
    places = jnp.arange(groups * capacity, dtype=jnp.int32)
    origin, turn = places // capacity, places % capacity
    places = jnp.where(turn == 0, origin, groups + origin * (capacity - 1) + turn - 1)
    earlier = (slot_ids[:, None] < slot_ids[None, :]) & full[:, None]
    position = jnp.sum(earlier.astype(jnp.int32), axis=0)
    wanted = jnp.arange(RECV_AGG, dtype=jnp.int32)
    wanted_match = (wanted[:, None] == position[None, :]) & full[None, :]
    order = jnp.sum(jnp.where(wanted_match, places[None, :], 0), axis=1)
    solved, means = [], []
    for chunk in range(capacity):
        base = chunk * groups
        pieces = []
        for d in range(ranks):
            solver = base + (me - d) % ranks * per_rank
            sources = lax.dynamic_slice_in_dim(slot_source, solver, per_rank, 0)
            piece = jnp.swapaxes(state[:, sources], 1, 2)
            pieces.append(shifted(piece, "vox", -d) if d else piece)
        mine = base + me * per_rank
        own_strain = lax.dynamic_slice_in_dim(slot_strain, mine, per_rank, 1)
        updated, mean = micro_solve(pieces, own_strain, moduli, tables)
        means.append(mean)
        slabs = [updated[0]] + [shifted(updated[d], "vox", d) for d in range(1, ranks)]
        slabs = jnp.swapaxes(by_rank(slabs, 2), 1, 2)
        solved.append(slabs)
    moved = [lax.all_to_all(solved[0], "macro", split_axis=1, concat_axis=1, tiled=True)]
    if capacity > 1:
        rest = jnp.stack(solved[1:], axis=2)
        rest = lax.all_to_all(rest, "macro", split_axis=1, concat_axis=1, tiled=True)
        moved.append(rest.reshape((7, -1) + rest.shape[3:]))
    own_mean = jnp.stack(means, axis=1)
    parts = [own_mean] + [shifted(own_mean, "vox", d) for d in range(1, ranks)]
    averaged = by_rank(parts, 2).reshape(6, capacity * groups)
    stress_plastic = jnp.dot(averaged, match_float, precision=FULL_PREC)
    stress = jnp.where(plastic[None, :], stress_plastic, elastic_stress(strain, elastic_moduli))
    forces = nodal_forces(stress, grad_ops, volume)
    assembled = jnp.einsum("iae,aen->in", forces, node_match, precision=FULL_PREC)
    returned_force = shifted(assembled[:, own_nodes:], "macro", -1)
    residual = (
        assembled[:, :own_nodes] + jnp.dot(returned_force, halo_match, precision=FULL_PREC) - load
    )
    return (residual, pick_rows(order, moved))


def solution(mesh):
    return jax.shard_map(
        local,
        mesh=mesh,
        in_specs=(
            P(None, "macro"),
            P(None, "macro"),
            P(None, "macro"),
            P("macro"),
            P(None, None, "macro"),
            P("macro"),
            P(None, "macro"),
            P("macro"),
            P("macro"),
            P(None, "macro", "vox", None),
            P(None, "vox", None),
        ),
        out_specs=(P(None, "macro"), P(None, "macro", "vox", None)),
        check_vma=False,
    )
```

```python
import functools
import math

import jax
import jax.numpy as jnp
import numpy as np
from jax import lax
from jax.experimental import pallas as pl
from jax.experimental.pallas import tpu as pltpu
from jax.sharding import PartitionSpec as P


RECV_AGG = 24
PLASTIC_MAX = 48
VOX_SIDE = 16
VOX_PLANE = 256
SWEEPS = 4
HALF = VOX_SIDE // 2

LAM_REF = 3.0
MU_REF = 3.0
FULL_PREC = lax.Precision.HIGHEST

ROOT = math.sqrt(0.5)
COS1 = math.cos(math.pi / 8)
COS3 = math.cos(3 * math.pi / 8)
PAIRS = [(i, j) for i in range(6) for j in range(i, 6)]


def shifted(block, axis, distance):
    devices = range(lax.axis_size(axis))
    route = [((i - distance) % len(devices), i) for i in devices]
    return lax.ppermute(block, axis, route)


def by_rank(pieces, axis):
    ranks = len(pieces)
    me = lax.axis_index("vox")
    if ranks == 2:
        straight = jnp.concatenate(pieces, axis=axis)
        return jnp.where(me == 0, straight, jnp.concatenate(pieces[::-1], axis=axis))
    order = (me - jnp.arange(ranks)) % ranks
    stacked = jnp.moveaxis(jnp.stack(pieces)[order], 0, axis)
    shape = list(pieces[0].shape)
    shape[axis] *= ranks
    return stacked.reshape(shape)


def green_tables():
    line = np.arange(VOX_SIDE)
    signed = np.where(line < HALF, line, line - VOX_SIDE).astype(np.float64)
    freq = np.stack(np.meshgrid(signed, signed, signed, indexing="ij"))
    norm = np.sum(freq * freq, axis=0)
    inverse = np.where(norm > 0, 1.0 / np.maximum(norm, 1.0), 0.0)
    coupling = (LAM_REF + MU_REF) / (LAM_REF + 2.0 * MU_REF)
    spots = [(0, 0), (1, 1), (2, 2), (1, 2), (0, 2), (0, 1)]
    table = np.zeros((6, 6) + norm.shape)
    for j, (a, b) in enumerate(spots):
        tau = np.zeros((3, 3))
        tau[a, b] = tau[b, a] = 1.0
        trac = np.einsum("ij,jxyz->ixyz", tau, freq)
        along = np.sum(freq * trac, axis=0) * inverse
        wave = (trac - coupling * along * freq) * inverse / MU_REF
        for i, (c, d) in enumerate(spots):
            table[i, j] = 0.5 * (freq[c] * wave[d] + freq[d] * wave[c])
    back = -line % VOX_SIDE
    flipped = table[:, :, back][:, :, :, back][:, :, :, :, back]
    even = 0.5 * (table + flipped) / VOX_SIDE**3
    even[:, 3:] *= 0.5
    stacked = np.stack([even[i, j] for i, j in PAIRS])
    return stacked.reshape(len(PAIRS), VOX_SIDE, VOX_PLANE).astype(np.float32)


def plane_tables():
    plane = np.arange(VOX_PLANE)
    rows, cols = plane // VOX_SIDE, plane % VOX_SIDE
    phase = (rows[:, None] * rows[None, :] + cols[:, None] * cols[None, :]) % VOX_SIDE
    angle = phase * (2.0 * math.pi / VOX_SIDE)
    plus = jnp.asarray((np.cos(angle) + np.sin(angle)).astype(np.float32))
    minus = jnp.asarray((np.cos(angle) - np.sin(angle)).astype(np.float32))
    out = []
    for table in (plus, minus):
        high = table.astype(jnp.bfloat16)
        out += [high, (table - high.astype(jnp.float32)).astype(jnp.bfloat16)]
    return jnp.stack(out)


def cosine_line(a):
    sums = [None] + [a[x] + a[8 - x] for x in (1, 2, 3)]
    diffs = [None] + [a[x] - a[8 - x] for x in (1, 2, 3)]
    even0, odd0 = a[0] + a[8], a[0] - a[8]
    outer, inner = even0 + a[4], even0 - a[4]
    spread = sums[1] + sums[3]
    slant = ROOT * (sums[1] - sums[3])
    mid = ROOT * diffs[2]
    first = COS1 * diffs[1] + COS3 * diffs[3]
    second = COS3 * diffs[1] - COS1 * diffs[3]
    top, low = odd0 + mid, odd0 - mid
    core = outer + sums[2]
    return [
        core + spread,
        top + first,
        inner + slant,
        low + second,
        outer - sums[2],
        low - second,
        inner - slant,
        top - first,
        core - spread,
    ]


def sine_line(b):
    sums = [None] + [b[x] + b[8 - x] for x in (1, 2, 3)]
    diffs = [None] + [b[x] - b[8 - x] for x in (1, 2, 3)]
    slant = ROOT * (diffs[1] + diffs[3])
    mid = ROOT * sums[2]
    first = COS3 * sums[1] + COS1 * sums[3]
    second = COS1 * sums[1] - COS3 * sums[3]
    return [
        None,
        (first + mid) + b[4],
        slant + diffs[2],
        (second + mid) - b[4],
        diffs[1] - diffs[3],
        (second - mid) + b[4],
        slant - diffs[2],
        (first - mid) - b[4],
    ]


def split_dot(block, table_ref, first):
    high = block.astype(jnp.bfloat16)
    low = (block - high.astype(jnp.float32)).astype(jnp.bfloat16)
    dot = functools.partial(jnp.dot, preferred_element_type=jnp.float32)
    return dot(high, table_ref[first]) + (dot(high, table_ref[first + 1]) + dot(low, table_ref[first]))


def voxel_law(strain, state_ref, props_ref, place, x):
    row = pl.ds(x, 1)
    lam, mu = props_ref[0, row, :], props_ref[1, row, :]
    yield_base, harden = props_ref[2, row, :], props_ref[3, row, :]
    two_mu, three_mu = 2.0 * mu, 3.0 * mu
    stiff_inv = 1.0 / (three_mu + harden)
    bulk = lam + two_mu * (1.0 / 3.0)
    elastic = [strain[c] - state_ref[c, place] for c in range(6)]
    trace = elastic[0] + elastic[1] + elastic[2]
    third = trace * (1.0 / 3.0)
    shape = [elastic[c] - third for c in range(3)] + elastic[3:]
    normal = shape[0] * shape[0] + shape[1] * shape[1] + shape[2] * shape[2]
    shear = shape[3] * shape[3] + shape[4] * shape[4] + shape[5] * shape[5]
    equivalent = two_mu * jnp.sqrt(1.5 * (normal + 2.0 * shear))
    strength = yield_base + harden * state_ref[6, place]
    gain = jnp.maximum(equivalent - strength, 0.0) * stiff_inv
    factor = gain / jnp.maximum(equivalent, strength)
    keep = two_mu * (1.0 - three_mu * factor)
    pressure = bulk * trace
    stress = [pressure + keep * shape[c] for c in range(3)] + [keep * shape[c] for c in range(3, 6)]
    return stress, shape, (1.5 * two_mu) * factor, gain


def solve_kernel(ranks, strain_ref, props_ref, green_ref, plane_ref, *refs):
    state_refs, new_refs = refs[:ranks], refs[ranks : 2 * ranks]
    mean_ref, eps, work, cos_ref, sin_ref = refs[2 * ranks :]
    thickness, rows = state_refs[0].shape[1:3]
    for c in range(6):
        start = jnp.broadcast_to(strain_ref[c], (VOX_SIDE, rows, VOX_PLANE))
        eps[c] = start

    def sweep(step, carry):
        for slab, state_ref in enumerate(state_refs):

            def law(place, inner, slab=slab, state_ref=state_ref):
                x = slab * thickness + place
                strain = [eps[c, x] for c in range(6)]
                stress = voxel_law(strain, state_ref, props_ref, place, x)[0]
                for c in range(6):
                    work[c, x] = stress[c]
                return inner

            lax.fori_loop(0, thickness, law, 0)

        def forward(c, inner):
            field = [work[c, x] for x in range(VOX_SIDE)]
            sums = [field[0]] + [field[x] + field[VOX_SIDE - x] for x in range(1, HALF)] + [field[HALF]]
            diffs = [None] + [field[x] - field[VOX_SIDE - x] for x in range(1, HALF)]
            for k, value in enumerate(cosine_line(sums)):
                cos_ref[c, k] = value
            for k, value in enumerate(sine_line(diffs)):
                if k > 0:
                    sin_ref[c, k - 1] = value
            return inner

        lax.fori_loop(0, 6, forward, 0)

        def plane():
            for ref, first in ((cos_ref, 0), (sin_ref, 2)):
                flat = ref[...].reshape(6 * ref.shape[1] * rows, VOX_PLANE)
                ref[...] = split_dot(flat, plane_ref, first).reshape(ref.shape)

        def apply(field, k):
            row = pl.ds(k, 1)
            field = field[:3] + [2.0 * field[c] for c in range(3, 6)]
            total = [None] * 6
            for n, (i, j) in enumerate(PAIRS):
                entry = green_ref[n, row, :]
                for a, b in [(i, j), (j, i)][: 1 + (i != j)]:
                    term = entry * field[b]
                    total[a] = term if total[a] is None else total[a] + term
            return total

        plane()
        for k in (0, HALF):
            result = apply([cos_ref[c, k] for c in range(6)], k)
            for c in range(6):
                cos_ref[c, k] = result[c]

        def mix(k, inner):
            even = [cos_ref[c, k] for c in range(6)]
            odd = [sin_ref[c, k - 1] for c in range(6)]
            ahead = apply([even[c] + odd[c] for c in range(6)], k)
            behind = apply([even[c] - odd[c] for c in range(6)], VOX_SIDE - k)
            for c in range(6):
                cos_ref[c, k] = ahead[c] + behind[c]
                sin_ref[c, k - 1] = ahead[c] - behind[c]
            return inner

        lax.fori_loop(1, HALF, mix, 0)
        plane()

        def backward(c, inner):
            even = cosine_line([cos_ref[c, k] for k in range(HALF + 1)])
            odd = sine_line([None] + [sin_ref[c, k - 1] for k in range(1, HALF)])
            eps[c, 0] = eps[c, 0] - even[0]
            eps[c, HALF] = eps[c, HALF] - even[HALF]
            for x in range(1, HALF):
                eps[c, x] = eps[c, x] - (even[x] + odd[x])
                eps[c, VOX_SIDE - x] = eps[c, VOX_SIDE - x] - (even[x] - odd[x])
            return inner

        lax.fori_loop(0, 6, backward, 0)
        return carry

    lax.fori_loop(0, SWEEPS, sweep, 0)
    zero = jnp.zeros((rows, VOX_PLANE), jnp.float32)
    totals = (zero,) * 6
    for slab, (state_ref, new_ref) in enumerate(zip(state_refs, new_refs)):

        def finish(place, totals, slab=slab, state_ref=state_ref, new_ref=new_ref):
            x = slab * thickness + place
            strain = [eps[c, x] for c in range(6)]
            stress, shape, scale, gain = voxel_law(strain, state_ref, props_ref, place, x)
            for c in range(6):
                new_ref[c, place] = state_ref[c, place] + scale * shape[c]
            new_ref[6, place] = state_ref[6, place] + gain
            return tuple(totals[c] + stress[c] for c in range(6))

        totals = lax.fori_loop(0, thickness, finish, totals)
    for c in range(6):
        total = jnp.sum(totals[c], axis=1, keepdims=True) / VOX_SIDE**3
        mean_ref[c] = jnp.broadcast_to(total, mean_ref.shape[1:])


def micro_solve(pieces, strains, moduli, tables):
    ranks = len(pieces)
    rows = pieces[0].shape[2]
    strain_rows = jnp.broadcast_to(strains[:, :, None], (6, rows, VOX_PLANE))
    vmem = pl.BlockSpec(memory_space=pltpu.VMEM)
    cells = VOX_SIDE * rows * VOX_PLANE
    results = pl.pallas_call(
        functools.partial(solve_kernel, ranks),
        out_shape=[jax.ShapeDtypeStruct(pieces[0].shape, jnp.float32)] * ranks
        + [jax.ShapeDtypeStruct((6, rows, 128), jnp.float32)],
        in_specs=[vmem] * (4 + ranks),
        out_specs=[vmem] * (ranks + 1),
        scratch_shapes=[
            pltpu.VMEM((6, VOX_SIDE, rows, VOX_PLANE), jnp.float32),
            pltpu.VMEM((6, VOX_SIDE, rows, VOX_PLANE), jnp.float32),
            pltpu.VMEM((6, HALF + 1, rows, VOX_PLANE), jnp.float32),
            pltpu.VMEM((6, HALF - 1, rows, VOX_PLANE), jnp.float32),
        ],
        compiler_params=pltpu.CompilerParams(vmem_limit_bytes=24 * 2**20),
        cost_estimate=pl.CostEstimate(
            flops=SWEEPS * 2 * 3 * 2 * 6 * cells * VOX_PLANE,
            bytes_accessed=2 * 7 * cells * 4,
            transcendentals=SWEEPS * cells,
        ),
    )(strain_rows, moduli, *tables, *pieces)
    return results[:ranks], results[ranks][:, :, 0]


def pick_kernel(order_ref, *refs):
    out_ref = refs[-1]

    def place(j, carry):
        low = 0
        for part in refs[:-1]:
            size = part.shape[1]
            spot = order_ref[j] - low

            @pl.when((spot >= 0) & (spot < size))
            def _(part=part, spot=spot):
                out_ref[:, j] = part[:, spot]

            low += size
        return carry

    lax.fori_loop(0, out_ref.shape[1], place, 0)


def pick_rows(order, parts):
    shape = (parts[0].shape[0], order.shape[0]) + parts[0].shape[2:]
    vmem = pl.BlockSpec(memory_space=pltpu.VMEM)
    return pl.pallas_call(
        pick_kernel,
        out_shape=jax.ShapeDtypeStruct(shape, jnp.float32),
        in_specs=[pl.BlockSpec(memory_space=pltpu.SMEM)] + [vmem] * len(parts),
        out_specs=vmem,
        compiler_params=pltpu.CompilerParams(vmem_limit_bytes=16 * 2**20),
    )(order, *parts)


def strain_tensor(disp_el, grad_el):
    products = [[jnp.sum(disp_el[i] * grad_el[j], axis=0) for j in range(3)] for i in range(3)]
    return jnp.stack(
        [
            products[0][0],
            products[1][1],
            products[2][2],
            0.5 * (products[1][2] + products[2][1]),
            0.5 * (products[0][2] + products[2][0]),
            0.5 * (products[0][1] + products[1][0]),
        ]
    )


def full_tensor(voigt):
    return [
        [voigt[0], voigt[5], voigt[4]],
        [voigt[5], voigt[1], voigt[3]],
        [voigt[4], voigt[3], voigt[2]],
    ]


def nodal_forces(stress, grad_el, volume):
    tensor = full_tensor(stress)
    return jnp.stack(
        [
            volume
            * (tensor[i][0] * grad_el[0] + tensor[i][1] * grad_el[1] + tensor[i][2] * grad_el[2])
            for i in range(3)
        ]
    )


def elastic_stress(strain, moduli):
    lame_first = moduli[0]
    shear_mod = moduli[1]
    trace = strain[0] + strain[1] + strain[2]
    return jnp.stack(
        [lame_first * trace + 2.0 * shear_mod * strain[c] for c in range(3)]
        + [2.0 * shear_mod * strain[c] for c in range(3, 6)]
    )


def local(
    displacement,
    load,
    conn,
    halo_list,
    grad_ops,
    volume,
    elastic_moduli,
    plastic_mask,
    new_owner,
    state,
    micro_moduli,
):
    groups = lax.axis_size("macro")
    ranks = lax.axis_size("vox")
    me = lax.axis_index("vox")
    own_nodes = displacement.shape[1]
    elements = conn.shape[1]
    per_rank = groups // ranks
    tables = (jnp.asarray(green_tables()), plane_tables())
    moduli = jnp.concatenate(
        [micro_moduli] + [shifted(micro_moduli, "vox", -d) for d in range(1, ranks)], axis=1
    )
    node_ids = jnp.arange(own_nodes, dtype=jnp.int32)
    halo_match = (halo_list[:, None] == node_ids[None, :]).astype(jnp.float32)
    halo_out = jnp.dot(displacement, halo_match.T, precision=FULL_PREC)
    halo_disp = shifted(halo_out, "macro", 1)
    local_disp = jnp.concatenate([displacement, halo_disp], axis=1)
    all_ids = jnp.arange(local_disp.shape[1], dtype=jnp.int32)
    node_match = (conn[:, :, None] == all_ids[None, None, :]).astype(jnp.float32)
    disp_el = jnp.einsum("in,aen->iae", local_disp, node_match, precision=FULL_PREC)
    strain = strain_tensor(disp_el, grad_ops)
    plastic = plastic_mask == 1
    point_ids = jnp.arange(elements, dtype=jnp.int32)
    same_owner = (
        (new_owner[:, None] == new_owner[None, :])
        & plastic[:, None]
        & plastic[None, :]
        & (point_ids[None, :] < point_ids[:, None])
    )
    owner_rank = jnp.sum(same_owner.astype(jnp.int32), axis=1)
    capacity = (PLASTIC_MAX + groups - 1) // groups
    send_slot = jnp.where(plastic, owner_rank * groups + new_owner, -1)
    slot_ids = jnp.arange(groups * capacity, dtype=jnp.int32)
    slot_match = slot_ids[:, None] == send_slot[None, :]
    match_float = slot_match.astype(jnp.float32)
    slot_valid = jnp.sum(match_float, axis=1)
    slot_source = jnp.sum(jnp.where(slot_match, point_ids[None, :], 0), axis=1)
    slot_strain = jnp.dot(strain, match_float.T, precision=FULL_PREC)
    here = capacity - 1 if capacity > 1 else capacity
    full_width = groups * here
    valid_rows = jnp.swapaxes(slot_valid.reshape(capacity, groups), 0, 1)
    if here < capacity:
        early = lax.all_to_all(
            state[:, slot_source[full_width:]], "macro", split_axis=1, concat_axis=1, tiled=True
        )
        valid_rows = jnp.concatenate([valid_rows, slot_strain[:, full_width:].T], axis=1)
    got_rows = lax.all_to_all(valid_rows, "macro", split_axis=0, concat_axis=0, tiled=True)
    full = got_rows[:, :capacity].reshape(-1) > 0.5
    places = slot_ids % capacity * groups + slot_ids // capacity
    earlier = (slot_ids[:, None] < slot_ids[None, :]) & full[:, None]
    position = jnp.sum(earlier.astype(jnp.int32), axis=0)
    wanted = jnp.arange(RECV_AGG, dtype=jnp.int32)
    wanted_match = (wanted[:, None] == position[None, :]) & full[None, :]
    order = jnp.sum(jnp.where(wanted_match, places[None, :], 0), axis=1)

    def solve_chunk(select, chunk_strain):
        pieces = []
        for d in range(ranks):
            piece = jnp.swapaxes(select((me - d) % ranks * per_rank), 1, 2)
            pieces.append(shifted(piece, "vox", -d) if d else piece)
        own_strain = lax.dynamic_slice_in_dim(chunk_strain, me * per_rank, per_rank, 1)
        updated, mean = micro_solve(pieces, own_strain, moduli, tables)
        slabs = [updated[0]] + [shifted(updated[d], "vox", d) for d in range(1, ranks)]
        return jnp.swapaxes(by_rank(slabs, 2), 1, 2), mean

    moved, means = [], []
    for chunk in range(here):
        base = chunk * groups

        def select(start, base=base):
            return state[:, lax.dynamic_slice_in_dim(slot_source, base + start, per_rank, 0)]

        slabs, mean = solve_chunk(select, slot_strain[:, base : base + groups])
        means.append(mean)
        moved.append(lax.all_to_all(slabs, "macro", split_axis=1, concat_axis=1, tiled=True))
    if here < capacity:

        def select(start):
            return lax.dynamic_slice_in_dim(early, start, per_rank, 1)

        slabs, mean = solve_chunk(select, got_rows[:, capacity:].T)
        means.append(mean)
        moved.append(slabs)
    own_mean = jnp.stack(means, axis=1)
    parts = [own_mean] + [shifted(own_mean, "vox", d) for d in range(1, ranks)]
    averaged = by_rank(parts, 2).reshape(6, capacity * groups)
    if here < capacity:
        returned = lax.all_to_all(
            averaged[:, full_width:].T, "macro", split_axis=0, concat_axis=0, tiled=True
        )
        averaged = jnp.concatenate([averaged[:, :full_width], returned.T], axis=1)
    stress_plastic = jnp.dot(averaged, match_float, precision=FULL_PREC)
    stress = jnp.where(plastic[None, :], stress_plastic, elastic_stress(strain, elastic_moduli))
    forces = nodal_forces(stress, grad_ops, volume)
    assembled = jnp.einsum("iae,aen->in", forces, node_match, precision=FULL_PREC)
    returned_force = shifted(assembled[:, own_nodes:], "macro", -1)
    residual = (
        assembled[:, :own_nodes] + jnp.dot(returned_force, halo_match, precision=FULL_PREC) - load
    )
    return (residual, pick_rows(order, moved))


def solution(mesh):
    return jax.shard_map(
        local,
        mesh=mesh,
        in_specs=(
            P(None, "macro"),
            P(None, "macro"),
            P(None, "macro"),
            P("macro"),
            P(None, None, "macro"),
            P("macro"),
            P(None, "macro"),
            P("macro"),
            P("macro"),
            P(None, "macro", "vox", None),
            P(None, "vox", None),
        ),
        out_specs=(P(None, "macro"), P(None, "macro", "vox", None)),
        check_vma=False,
    )
```

```python
import functools
import math

import jax
import jax.numpy as jnp
import numpy as np
from jax import lax
from jax.experimental import pallas as pl
from jax.experimental.pallas import tpu as pltpu
from jax.sharding import PartitionSpec as P


RECV_AGG = 24
PLASTIC_MAX = 48
VOX_SIDE = 16
VOX_PLANE = 256
SWEEPS = 4
HALF = VOX_SIDE // 2

LAM_REF = 3.0
MU_REF = 3.0
FULL_PREC = lax.Precision.HIGHEST

ROOT = math.sqrt(0.5)
COS1 = math.cos(math.pi / 8)
COS3 = math.cos(3 * math.pi / 8)
PAIRS = [(i, j) for i in range(6) for j in range(i, 6)]


def shifted(block, axis, distance):
    devices = range(lax.axis_size(axis))
    route = [((i - distance) % len(devices), i) for i in devices]
    return lax.ppermute(block, axis, route)


def by_rank(pieces, axis):
    ranks = len(pieces)
    me = lax.axis_index("vox")
    if ranks == 2:
        straight = jnp.concatenate(pieces, axis=axis)
        return jnp.where(me == 0, straight, jnp.concatenate(pieces[::-1], axis=axis))
    order = (me - jnp.arange(ranks)) % ranks
    stacked = jnp.moveaxis(jnp.stack(pieces)[order], 0, axis)
    shape = list(pieces[0].shape)
    shape[axis] *= ranks
    return stacked.reshape(shape)


def green_tables():
    line = np.arange(VOX_SIDE)
    signed = np.where(line < HALF, line, line - VOX_SIDE).astype(np.float64)
    freq = np.stack(np.meshgrid(signed, signed, signed, indexing="ij"))
    norm = np.sum(freq * freq, axis=0)
    inverse = np.where(norm > 0, 1.0 / np.maximum(norm, 1.0), 0.0)
    coupling = (LAM_REF + MU_REF) / (LAM_REF + 2.0 * MU_REF)
    spots = [(0, 0), (1, 1), (2, 2), (1, 2), (0, 2), (0, 1)]
    table = np.zeros((6, 6) + norm.shape)
    for j, (a, b) in enumerate(spots):
        tau = np.zeros((3, 3))
        tau[a, b] = tau[b, a] = 1.0
        trac = np.einsum("ij,jxyz->ixyz", tau, freq)
        along = np.sum(freq * trac, axis=0) * inverse
        wave = (trac - coupling * along * freq) * inverse / MU_REF
        for i, (c, d) in enumerate(spots):
            table[i, j] = 0.5 * (freq[c] * wave[d] + freq[d] * wave[c])
    back = -line % VOX_SIDE
    flipped = table[:, :, back][:, :, :, back][:, :, :, :, back]
    even = 0.5 * (table + flipped) / VOX_SIDE**3
    even[:, 3:] *= 0.5
    stacked = np.stack([even[i, j] for i, j in PAIRS])
    return stacked.reshape(len(PAIRS), VOX_SIDE, VOX_PLANE).astype(np.float32)


def plane_tables():
    plane = np.arange(VOX_PLANE)
    rows, cols = plane // VOX_SIDE, plane % VOX_SIDE
    phase = (rows[:, None] * rows[None, :] + cols[:, None] * cols[None, :]) % VOX_SIDE
    angle = phase * (2.0 * math.pi / VOX_SIDE)
    plus = jnp.asarray((np.cos(angle) + np.sin(angle)).astype(np.float32))
    minus = jnp.asarray((np.cos(angle) - np.sin(angle)).astype(np.float32))
    out = []
    for table in (plus, minus):
        high = table.astype(jnp.bfloat16)
        out += [high, (table - high.astype(jnp.float32)).astype(jnp.bfloat16)]
    return jnp.stack(out)


def cosine_line(a):
    sums = [None] + [a[x] + a[8 - x] for x in (1, 2, 3)]
    diffs = [None] + [a[x] - a[8 - x] for x in (1, 2, 3)]
    even0, odd0 = a[0] + a[8], a[0] - a[8]
    outer, inner = even0 + a[4], even0 - a[4]
    spread = sums[1] + sums[3]
    slant = ROOT * (sums[1] - sums[3])
    mid = ROOT * diffs[2]
    first = COS1 * diffs[1] + COS3 * diffs[3]
    second = COS3 * diffs[1] - COS1 * diffs[3]
    top, low = odd0 + mid, odd0 - mid
    core = outer + sums[2]
    return [
        core + spread,
        top + first,
        inner + slant,
        low + second,
        outer - sums[2],
        low - second,
        inner - slant,
        top - first,
        core - spread,
    ]


def sine_line(b):
    sums = [None] + [b[x] + b[8 - x] for x in (1, 2, 3)]
    diffs = [None] + [b[x] - b[8 - x] for x in (1, 2, 3)]
    slant = ROOT * (diffs[1] + diffs[3])
    mid = ROOT * sums[2]
    first = COS3 * sums[1] + COS1 * sums[3]
    second = COS1 * sums[1] - COS3 * sums[3]
    return [
        None,
        (first + mid) + b[4],
        slant + diffs[2],
        (second + mid) - b[4],
        diffs[1] - diffs[3],
        (second - mid) + b[4],
        slant - diffs[2],
        (first - mid) - b[4],
    ]


def split_dot(block, table_ref, first):
    high = block.astype(jnp.bfloat16)
    low = (block - high.astype(jnp.float32)).astype(jnp.bfloat16)
    dot = functools.partial(jnp.dot, preferred_element_type=jnp.float32)
    return dot(high, table_ref[first]) + (dot(high, table_ref[first + 1]) + dot(low, table_ref[first]))


def voxel_law(strain, state_ref, props_ref, place, x):
    row = pl.ds(x, 1)
    lam, mu = props_ref[0, row, :], props_ref[1, row, :]
    yield_base, harden = props_ref[2, row, :], props_ref[3, row, :]
    two_mu, three_mu = 2.0 * mu, 3.0 * mu
    stiff_inv = 1.0 / (three_mu + harden)
    bulk = lam + two_mu * (1.0 / 3.0)
    elastic = [strain[c] - state_ref[c, place] for c in range(6)]
    trace = elastic[0] + elastic[1] + elastic[2]
    third = trace * (1.0 / 3.0)
    shape = [elastic[c] - third for c in range(3)] + elastic[3:]
    normal = shape[0] * shape[0] + shape[1] * shape[1] + shape[2] * shape[2]
    shear = shape[3] * shape[3] + shape[4] * shape[4] + shape[5] * shape[5]
    equivalent = two_mu * jnp.sqrt(1.5 * (normal + 2.0 * shear))
    strength = yield_base + harden * state_ref[6, place]
    gain = jnp.maximum(equivalent - strength, 0.0) * stiff_inv
    factor = gain / jnp.maximum(equivalent, strength)
    keep = two_mu * (1.0 - three_mu * factor)
    pressure = bulk * trace
    stress = [pressure + keep * shape[c] for c in range(3)] + [keep * shape[c] for c in range(3, 6)]
    return stress, shape, (1.5 * two_mu) * factor, gain


def solve_kernel(ranks, strain_ref, props_ref, green_ref, plane_ref, *refs):
    state_refs, new_refs = refs[:ranks], refs[ranks : 2 * ranks]
    mean_ref, eps, work, cos_ref, sin_ref = refs[2 * ranks :]
    thickness, rows = state_refs[0].shape[1:3]
    for c in range(6):
        start = jnp.broadcast_to(strain_ref[c], (VOX_SIDE, rows, VOX_PLANE))
        eps[c] = start

    def sweep(step, carry):
        for slab, state_ref in enumerate(state_refs):

            def law(place, inner, slab=slab, state_ref=state_ref):
                x = slab * thickness + place
                strain = [eps[c, x] for c in range(6)]
                stress = voxel_law(strain, state_ref, props_ref, place, x)[0]
                for c in range(6):
                    work[c, x] = stress[c]
                return inner

            lax.fori_loop(0, thickness, law, 0)

        def forward(c, inner):
            field = [work[c, x] for x in range(VOX_SIDE)]
            sums = [field[0]] + [field[x] + field[VOX_SIDE - x] for x in range(1, HALF)] + [field[HALF]]
            diffs = [None] + [field[x] - field[VOX_SIDE - x] for x in range(1, HALF)]
            for k, value in enumerate(cosine_line(sums)):
                cos_ref[c, k] = value
            for k, value in enumerate(sine_line(diffs)):
                if k > 0:
                    sin_ref[c, k - 1] = value
            return inner

        lax.fori_loop(0, 6, forward, 0)

        def plane():
            for ref, first in ((cos_ref, 0), (sin_ref, 2)):
                flat = ref[...].reshape(6 * ref.shape[1] * rows, VOX_PLANE)
                ref[...] = split_dot(flat, plane_ref, first).reshape(ref.shape)

        def apply(field, k):
            row = pl.ds(k, 1)
            field = field[:3] + [2.0 * field[c] for c in range(3, 6)]
            total = [None] * 6
            for n, (i, j) in enumerate(PAIRS):
                entry = green_ref[n, row, :]
                for a, b in [(i, j), (j, i)][: 1 + (i != j)]:
                    term = entry * field[b]
                    total[a] = term if total[a] is None else total[a] + term
            return total

        plane()
        for k in (0, HALF):
            result = apply([cos_ref[c, k] for c in range(6)], k)
            for c in range(6):
                cos_ref[c, k] = result[c]

        def mix(k, inner):
            even = [cos_ref[c, k] for c in range(6)]
            odd = [sin_ref[c, k - 1] for c in range(6)]
            ahead = apply([even[c] + odd[c] for c in range(6)], k)
            behind = apply([even[c] - odd[c] for c in range(6)], VOX_SIDE - k)
            for c in range(6):
                cos_ref[c, k] = ahead[c] + behind[c]
                sin_ref[c, k - 1] = ahead[c] - behind[c]
            return inner

        lax.fori_loop(1, HALF, mix, 0)
        plane()

        def backward(c, inner):
            even = cosine_line([cos_ref[c, k] for k in range(HALF + 1)])
            odd = sine_line([None] + [sin_ref[c, k - 1] for k in range(1, HALF)])
            eps[c, 0] = eps[c, 0] - even[0]
            eps[c, HALF] = eps[c, HALF] - even[HALF]
            for x in range(1, HALF):
                eps[c, x] = eps[c, x] - (even[x] + odd[x])
                eps[c, VOX_SIDE - x] = eps[c, VOX_SIDE - x] - (even[x] - odd[x])
            return inner

        lax.fori_loop(0, 6, backward, 0)
        return carry

    lax.fori_loop(0, SWEEPS, sweep, 0)
    zero = jnp.zeros((rows, VOX_PLANE), jnp.float32)
    totals = (zero,) * 6
    for slab, (state_ref, new_ref) in enumerate(zip(state_refs, new_refs)):

        def finish(place, totals, slab=slab, state_ref=state_ref, new_ref=new_ref):
            x = slab * thickness + place
            strain = [eps[c, x] for c in range(6)]
            stress, shape, scale, gain = voxel_law(strain, state_ref, props_ref, place, x)
            for c in range(6):
                new_ref[c, place] = state_ref[c, place] + scale * shape[c]
            new_ref[6, place] = state_ref[6, place] + gain
            return tuple(totals[c] + stress[c] for c in range(6))

        totals = lax.fori_loop(0, thickness, finish, totals)
    for c in range(6):
        total = jnp.sum(totals[c], axis=1, keepdims=True) / VOX_SIDE**3
        mean_ref[c] = jnp.broadcast_to(total, mean_ref.shape[1:])


def micro_solve(pieces, strains, moduli, tables):
    ranks = len(pieces)
    rows = pieces[0].shape[2]
    strain_rows = jnp.broadcast_to(strains[:, :, None], (6, rows, VOX_PLANE))
    vmem = pl.BlockSpec(memory_space=pltpu.VMEM)
    cells = VOX_SIDE * rows * VOX_PLANE
    results = pl.pallas_call(
        functools.partial(solve_kernel, ranks),
        out_shape=[jax.ShapeDtypeStruct(pieces[0].shape, jnp.float32)] * ranks
        + [jax.ShapeDtypeStruct((6, rows, 128), jnp.float32)],
        in_specs=[vmem] * (4 + ranks),
        out_specs=[vmem] * (ranks + 1),
        scratch_shapes=[
            pltpu.VMEM((6, VOX_SIDE, rows, VOX_PLANE), jnp.float32),
            pltpu.VMEM((6, VOX_SIDE, rows, VOX_PLANE), jnp.float32),
            pltpu.VMEM((6, HALF + 1, rows, VOX_PLANE), jnp.float32),
            pltpu.VMEM((6, HALF - 1, rows, VOX_PLANE), jnp.float32),
        ],
        compiler_params=pltpu.CompilerParams(vmem_limit_bytes=24 * 2**20),
        cost_estimate=pl.CostEstimate(
            flops=SWEEPS * 2 * 3 * 2 * 6 * cells * VOX_PLANE,
            bytes_accessed=2 * 7 * cells * 4,
            transcendentals=SWEEPS * cells,
        ),
    )(strain_rows, moduli, *tables, *pieces)
    return results[:ranks], results[ranks][:, :, 0]


def pick_kernel(order_ref, *refs):
    out_ref = refs[-1]

    def place(j, carry):
        low = 0
        for part in refs[:-1]:
            size = part.shape[1]
            spot = order_ref[j] - low

            @pl.when((spot >= 0) & (spot < size))
            def _(part=part, spot=spot):
                out_ref[:, j] = part[:, spot]

            low += size
        return carry

    lax.fori_loop(0, out_ref.shape[1], place, 0)


def pick_rows(order, parts):
    shape = (parts[0].shape[0], order.shape[0]) + parts[0].shape[2:]
    vmem = pl.BlockSpec(memory_space=pltpu.VMEM)
    return pl.pallas_call(
        pick_kernel,
        out_shape=jax.ShapeDtypeStruct(shape, jnp.float32),
        in_specs=[pl.BlockSpec(memory_space=pltpu.SMEM)] + [vmem] * len(parts),
        out_specs=vmem,
        compiler_params=pltpu.CompilerParams(vmem_limit_bytes=16 * 2**20),
    )(order, *parts)


def strain_tensor(disp_el, grad_el):
    products = [[jnp.sum(disp_el[i] * grad_el[j], axis=0) for j in range(3)] for i in range(3)]
    return jnp.stack(
        [
            products[0][0],
            products[1][1],
            products[2][2],
            0.5 * (products[1][2] + products[2][1]),
            0.5 * (products[0][2] + products[2][0]),
            0.5 * (products[0][1] + products[1][0]),
        ]
    )


def full_tensor(voigt):
    return [
        [voigt[0], voigt[5], voigt[4]],
        [voigt[5], voigt[1], voigt[3]],
        [voigt[4], voigt[3], voigt[2]],
    ]


def nodal_forces(stress, grad_el, volume):
    tensor = full_tensor(stress)
    return jnp.stack(
        [
            volume
            * (tensor[i][0] * grad_el[0] + tensor[i][1] * grad_el[1] + tensor[i][2] * grad_el[2])
            for i in range(3)
        ]
    )


def elastic_stress(strain, moduli):
    lame_first = moduli[0]
    shear_mod = moduli[1]
    trace = strain[0] + strain[1] + strain[2]
    return jnp.stack(
        [lame_first * trace + 2.0 * shear_mod * strain[c] for c in range(3)]
        + [2.0 * shear_mod * strain[c] for c in range(3, 6)]
    )


def local(
    displacement,
    load,
    conn,
    halo_list,
    grad_ops,
    volume,
    elastic_moduli,
    plastic_mask,
    new_owner,
    state,
    micro_moduli,
):
    groups = lax.axis_size("macro")
    ranks = lax.axis_size("vox")
    me = lax.axis_index("vox")
    own_nodes = displacement.shape[1]
    elements = conn.shape[1]
    per_rank = groups // ranks
    tables = (jnp.asarray(green_tables()), plane_tables())
    moduli = jnp.concatenate(
        [micro_moduli] + [shifted(micro_moduli, "vox", -d) for d in range(1, ranks)], axis=1
    )
    node_ids = jnp.arange(own_nodes, dtype=jnp.int32)
    halo_match = (halo_list[:, None] == node_ids[None, :]).astype(jnp.float32)
    halo_out = jnp.dot(displacement, halo_match.T, precision=FULL_PREC)
    halo_disp = shifted(halo_out, "macro", 1)
    local_disp = jnp.concatenate([displacement, halo_disp], axis=1)
    all_ids = jnp.arange(local_disp.shape[1], dtype=jnp.int32)
    node_match = (conn[:, :, None] == all_ids[None, None, :]).astype(jnp.float32)
    disp_el = jnp.einsum("in,aen->iae", local_disp, node_match, precision=FULL_PREC)
    strain = strain_tensor(disp_el, grad_ops)
    plastic = plastic_mask == 1
    point_ids = jnp.arange(elements, dtype=jnp.int32)
    same_owner = (
        (new_owner[:, None] == new_owner[None, :])
        & plastic[:, None]
        & plastic[None, :]
        & (point_ids[None, :] < point_ids[:, None])
    )
    owner_rank = jnp.sum(same_owner.astype(jnp.int32), axis=1)
    capacity = (PLASTIC_MAX + groups - 1) // groups
    send_slot = jnp.where(plastic, owner_rank * groups + new_owner, -1)
    slot_ids = jnp.arange(groups * capacity, dtype=jnp.int32)
    slot_match = slot_ids[:, None] == send_slot[None, :]
    match_float = slot_match.astype(jnp.float32)
    slot_valid = jnp.sum(match_float, axis=1)
    slot_source = jnp.sum(jnp.where(slot_match, point_ids[None, :], 0), axis=1)
    slot_strain = jnp.dot(strain, match_float.T, precision=FULL_PREC)
    here = capacity - 1 if capacity > 1 else capacity
    full_width = groups * here
    valid_rows = jnp.swapaxes(slot_valid.reshape(capacity, groups), 0, 1)
    if here < capacity:
        early = lax.all_to_all(
            state[:, slot_source[full_width:]], "macro", split_axis=1, concat_axis=1, tiled=True
        )
        valid_rows = jnp.concatenate([valid_rows, slot_strain[:, full_width:].T], axis=1)
    got_rows = lax.all_to_all(valid_rows, "macro", split_axis=0, concat_axis=0, tiled=True)
    full = got_rows[:, :capacity].reshape(-1) > 0.5
    places = slot_ids % capacity * groups + slot_ids // capacity
    earlier = (slot_ids[:, None] < slot_ids[None, :]) & full[:, None]
    position = jnp.sum(earlier.astype(jnp.int32), axis=0)
    wanted = jnp.arange(RECV_AGG, dtype=jnp.int32)
    wanted_match = (wanted[:, None] == position[None, :]) & full[None, :]
    order = jnp.sum(jnp.where(wanted_match, places[None, :], 0), axis=1)

    def solve_chunk(select, chunk_strain):
        pieces = []
        for d in range(ranks):
            piece = jnp.swapaxes(select((me - d) % ranks * per_rank), 1, 2)
            pieces.append(shifted(piece, "vox", -d) if d else piece)
        own_strain = lax.dynamic_slice_in_dim(chunk_strain, me * per_rank, per_rank, 1)
        updated, mean = micro_solve(pieces, own_strain, moduli, tables)
        slabs = [updated[0]] + [shifted(updated[d], "vox", d) for d in range(1, ranks)]
        return jnp.swapaxes(by_rank(slabs, 2), 1, 2), mean

    moved, means = [], []
    for chunk in range(here):
        base = chunk * groups

        def select(start, base=base):
            return state[:, lax.dynamic_slice_in_dim(slot_source, base + start, per_rank, 0)]

        slabs, mean = solve_chunk(select, slot_strain[:, base : base + groups])
        means.append(mean)
        moved.append(lax.all_to_all(slabs, "macro", split_axis=1, concat_axis=1, tiled=True))
    if here < capacity:

        def select(start):
            return lax.dynamic_slice_in_dim(early, start, per_rank, 1)

        slabs, mean = solve_chunk(select, got_rows[:, capacity:].T)
        means.append(mean)
        moved.append(slabs)
    own_mean = jnp.stack(means[:here], axis=1)
    parts = [own_mean] + [shifted(own_mean, "vox", d) for d in range(1, ranks)]
    averaged = by_rank(parts, 2).reshape(6, full_width)
    if here < capacity:
        parts = [means[here]] + [shifted(means[here], "vox", d) for d in range(1, ranks)]
        returned = lax.all_to_all(
            by_rank(parts, 1).T, "macro", split_axis=0, concat_axis=0, tiled=True
        )
        averaged = jnp.concatenate([averaged, returned.T], axis=1)
    stress_plastic = jnp.dot(averaged, match_float, precision=FULL_PREC)
    stress = jnp.where(plastic[None, :], stress_plastic, elastic_stress(strain, elastic_moduli))
    forces = nodal_forces(stress, grad_ops, volume)
    assembled = jnp.einsum("iae,aen->in", forces, node_match, precision=FULL_PREC)
    returned_force = shifted(assembled[:, own_nodes:], "macro", -1)
    residual = (
        assembled[:, :own_nodes] + jnp.dot(returned_force, halo_match, precision=FULL_PREC) - load
    )
    return (residual, pick_rows(order, moved))


def solution(mesh):
    return jax.shard_map(
        local,
        mesh=mesh,
        in_specs=(
            P(None, "macro"),
            P(None, "macro"),
            P(None, "macro"),
            P("macro"),
            P(None, None, "macro"),
            P("macro"),
            P(None, "macro"),
            P("macro"),
            P("macro"),
            P(None, "macro", "vox", None),
            P(None, "vox", None),
        ),
        out_specs=(P(None, "macro"), P(None, "macro", "vox", None)),
        check_vma=False,
    )
```
